32 devices in a mesh: grp: 4 (over x, core), cl: 8 (over z, y).
Axes of the slice: x: 2, y: 2, z: 4, core: 2. Of those that a mesh axis runs over, the one named last changes fastest.
Arguments:
- incident: float32 [16, 128, 512], P('cl', None, 'grp'), may hold values from -6 to 6
- near_real: float32 [16, 16, 128, 128], P('cl'), may hold values from -0.0625 to 0.0625
- near_imag: float32 [16, 16, 128, 128], P('cl'), may hold values from -0.0625 to 0.0625
- to_moments: float32 [16, 128, 128], P('cl'), may hold values from -0.5 to 0.5
- from_locals: float32 [16, 128, 128], P('cl'), may hold values from -0.25 to 0.25
- transfer_ops: float32 [16, 128, 128], replicated, may hold values from -0.09375 to 0.09375
- near_index: int32 [16, 16], P('cl'), may hold values from 0 to 5
- near_count: int32 [16], P('cl'), may hold values from 1 to 16
- cluster_box: int32 [16], P('cl'), may hold values from 0 to 1
- far_source: int32 [16, 32], P('cl'), may hold values from 0 to 15
- far_kind: int32 [16, 32], P('cl'), may hold values from 0 to 15
- far_count: int32 [16], P('cl'), may hold values from 8 to 32
Outputs:
- pressure: float32 [16, 128, 512], P('cl', None, 'grp')
- residual: float32 [16, 128, 512], P('cl', None, 'grp')
The draws below stay inside these ranges and needn't reach their ends.
Inputs may be any that keep to these rules, and one draw needn't show every extreme that they name: `near_index`: positions 0 to 1 are the clusters of the previous slab along cl (wrapping), then this slab's, then the next slab's. `far_source`: global box numbers.
All inputs are finite; a program needn't handle non-finite values.
Results may differ from the reference program's by a relative error of at most 0.0003.
Values sent between devices are 32-bit elements; how exact they have to be, the bound alone decides.
A program may use at most 64 MiB of HBM per device.

```python
import jax
import jax.numpy as jnp
from jax import lax

DIRS = 512
POINTS = 128
COEFFS = 128
CL_DEV = 2
BOX_DEV = 2
NEAR_MAX = 16
FAR_MAX = 32
KINDS = 16
ITERS = 2
CLUSTERS = 16
BOXES = 16
N_CL = 8


def set_ends(values, own_key, smallest, high):
    index_at = [jax.random.randint(jax.random.fold_in(own_key, axis), (), 0, length) for axis, length in enumerate(values.shape)]
    longest = values.shape.index(max(values.shape))
    neighbour = index_at[:longest] + [(index_at[longest] + 1) % values.shape[longest]] + index_at[longest + 1:]
    return values.at[tuple(index_at)].set(smallest).at[tuple(neighbour)].set(high)


def level_of(stream_key, dims, split, low, high):
    factor_of = 1.0
    for position, parts in split:
        draws = jax.random.uniform(jax.random.fold_in(jax.random.fold_in(stream_key, 6), position), (parts,), jnp.float32, low / len(split), high / len(split))
        factor_of = factor_of * jnp.repeat(jnp.exp(draws), dims[position] // parts).reshape((-1,) + (1,) * (len(dims) - 1 - position))
    return factor_of


def centred(own_key, extent, spread, limit, split=(), kind=jnp.bfloat16):
    entries = jax.random.normal(own_key, extent, jnp.float32) * spread
    if len(split) > 0:
        entries = level_of(own_key, extent, split, -0.22, 0.18) * entries
    return jnp.clip(entries, min=-limit, max=limit).astype(kind)


def setup_inputs(seed: int = 0) -> dict:
    arg_keys = jax.random.split(jax.random.key(seed), 13)
    incident = centred(arg_keys[0], (CLUSTERS, POINTS, DIRS), 1.0, 6.0, ((0, 8), (2, 4)), jnp.float32)
    near_real = centred(arg_keys[1], (CLUSTERS, NEAR_MAX, POINTS, POINTS), (4 * POINTS * NEAR_MAX) ** -0.5, 0.0625, ((0, 8),), jnp.float32)
    near_imag = centred(arg_keys[2], (CLUSTERS, NEAR_MAX, POINTS, POINTS), (4 * POINTS * NEAR_MAX) ** -0.5, 0.0625, ((0, 8),), jnp.float32)
    to_moments = centred(arg_keys[3], (CLUSTERS, COEFFS, POINTS), POINTS ** -0.5, 0.5, ((0, 8),), jnp.float32)
    from_locals = centred(arg_keys[4], (CLUSTERS, POINTS, COEFFS), (4 * COEFFS) ** -0.5, 0.25, ((0, 8),), jnp.float32)
    transfer_ops = centred(arg_keys[5], (KINDS, COEFFS, COEFFS), (COEFFS * FAR_MAX) ** -0.5, 0.09375, (), jnp.float32)
    near_index = set_ends(jax.random.randint(arg_keys[6], (CLUSTERS, NEAR_MAX), 0, 3 * CL_DEV), jax.random.fold_in(arg_keys[6], 1), 0, (3 * CL_DEV) - 1).astype(jnp.int32)
    near_count = set_ends(jax.random.randint(arg_keys[7], (CLUSTERS,), 1, NEAR_MAX + 1), jax.random.fold_in(arg_keys[7], 1), 1, NEAR_MAX).astype(jnp.int32)
    cluster_box = set_ends(jax.random.randint(arg_keys[8], (CLUSTERS,), 0, BOX_DEV), jax.random.fold_in(arg_keys[8], 1), 0, BOX_DEV - 1).astype(jnp.int32)
    far_source = set_ends(jax.random.randint(arg_keys[9], (BOXES, FAR_MAX), 0, BOXES), jax.random.fold_in(arg_keys[9], 1), 0, BOXES - 1).astype(jnp.int32)
    far_kind = set_ends(jax.random.randint(arg_keys[10], (BOXES, FAR_MAX), 0, KINDS), jax.random.fold_in(arg_keys[10], 1), 0, KINDS - 1).astype(jnp.int32)
    far_count = set_ends(jax.random.randint(arg_keys[11], (BOXES,), FAR_MAX // 4, FAR_MAX + 1), jax.random.fold_in(arg_keys[11], 1), FAR_MAX // 4, FAR_MAX).astype(jnp.int32)
    return dict(incident=incident, near_real=near_real, near_imag=near_imag, to_moments=to_moments, from_locals=from_locals, transfer_ops=transfer_ops, near_index=near_index, near_count=near_count, cluster_box=cluster_box, far_source=far_source, far_kind=far_kind, far_count=far_count)


DAMPING = 0.7


def operator_product(form, left, right):
    return jnp.einsum(form, left, right, precision=lax.Precision.HIGHEST)


def near_apply(iterate, near_real, near_imag, near_index, near_count):
    clusters, points, width = iterate.shape
    half = width // 2
    rotated_result = jnp.concatenate([-iterate[:, :, half:], iterate[:, :, :half]], axis=2)

    def one_block(inputs):
        block_index, real_blocks, imag_blocks, indices, counts = inputs
        sources = jnp.mod((block_index - 1) * CL_DEV + indices, clusters).astype(jnp.int32)
        live = (jnp.arange(NEAR_MAX, dtype=jnp.int32)[None, :] < counts[:, None]).astype(iterate.dtype)
        plain = jnp.take(iterate, sources, axis=0) * live[:, :, None, None]
        crossed = jnp.take(rotated_result, sources, axis=0) * live[:, :, None, None]
        return operator_product("cepq,ceqk->cpk", real_blocks, plain) + operator_product("cepq,ceqk->cpk", imag_blocks, crossed)

    inputs = (jnp.arange(N_CL, dtype=jnp.int32),
              near_real.reshape(N_CL, CL_DEV, NEAR_MAX, points, points),
              near_imag.reshape(N_CL, CL_DEV, NEAR_MAX, points, points),
              near_index.reshape(N_CL, CL_DEV, NEAR_MAX),
              near_count.reshape(N_CL, CL_DEV))
    return lax.map(one_block, inputs).reshape(clusters, points, width)


def far_apply(iterate, to_moments, from_locals, transfer_ops, cluster_box, far_source, far_kind, far_count):
    owner = ((jnp.arange(CLUSTERS, dtype=jnp.int32) // CL_DEV) * BOX_DEV + cluster_box).astype(jnp.int32)
    multipole_series = operator_product("cqp,cpk->cqk", to_moments, iterate)
    moment_values = jax.ops.segment_sum(multipole_series, owner, num_segments=BOXES)

    def one_target(inputs):
        sources, kinds, counts = inputs
        live = (jnp.arange(FAR_MAX, dtype=jnp.int32) < counts).astype(iterate.dtype)
        operators = jnp.take(transfer_ops, kinds, axis=0) * live[:, None, None]
        return operator_product("frq,fqk->rk", operators, jnp.take(moment_values, sources, axis=0))

    local_field = lax.map(one_target, (far_source, far_kind, far_count))
    return operator_product("cpr,crk->cpk", from_locals, jnp.take(local_field, owner, axis=0))


def reference(incident, near_real, near_imag, to_moments, from_locals, transfer_ops, near_index, near_count, cluster_box, far_source, far_kind, far_count):
    pressure = incident
    residual = jnp.zeros_like(incident)
    for iteration in range(ITERS):
        applied = pressure + near_apply(pressure, near_real, near_imag, near_index, near_count)
        applied = applied + far_apply(pressure, to_moments, from_locals, transfer_ops, cluster_box, far_source, far_kind, far_count)
        residual = incident - applied
        pressure = pressure + DAMPING * residual
    return pressure, residual
```

```python
import functools

import jax
import jax.numpy as jnp
from jax import lax
from jax.experimental import pallas as pl
from jax.experimental.pallas import tpu as pltpu
from jax.sharding import PartitionSpec as P

ITERS = 2


DAMPING = 0.7


def padded(block, sides, width):
    for axis, dim in sides:
        count = lax.axis_size(axis)
        forward = [(i, i + 1) for i in range(count - 1)]
        forward.append((count - 1, 0))
        backward = [(target, source) for source, target in forward]
        low = lax.ppermute(
            lax.slice_in_dim(block, block.shape[dim] - width, None, axis=dim), axis, forward
        )
        high = lax.ppermute(lax.slice_in_dim(block, 0, width, axis=dim), axis, backward)
        block = jnp.concatenate([low, block, high], axis=dim)
    return block


def partner(x, axis, bit):
    return lax.ppermute(x, axis, [(i, i ^ 1 << bit) for i in range(lax.axis_size(axis))])


def operator_product(form, left, right):
    return jnp.einsum(form, left, right, precision=lax.Precision.HIGHEST)


def shards(
    incident,
    near_real,
    near_imag,
    to_moments,
    from_locals,
    transfer_ops,
    near_index,
    near_count,
    cluster_box,
    far_source,
    far_kind,
    far_count,
):
    per_slab, points, width = incident.shape
    box_count, far_max = far_source.shape
    kind_total, coeffs = (transfer_ops.shape[0], transfer_ops.shape[1])
    near_max = near_index.shape[1]
    parity = jnp.where(lax.axis_index("grp") < lax.axis_size("grp") // 2, -1.0, 1.0).astype(
        jnp.float32
    )
    partner_bit = lax.axis_size("grp").bit_length() - 2
    live_near = (jnp.arange(near_max, dtype=jnp.int32)[None, :] < near_count[:, None]).astype(
        jnp.float32
    )
    window_hot = (
        near_index[:, :, None] == jnp.arange(3 * per_slab, dtype=jnp.int32)
    ).astype(jnp.float32) * live_near[:, :, None]
    box_onehot_matrix = (
        cluster_box[:, None] == jnp.arange(box_count, dtype=jnp.int32)[None, :]
    ).astype(jnp.float32)
    active_far_links = jnp.arange(far_max, dtype=jnp.int32)[None, :] < far_count[:, None]
    kind_hot = (
        (far_kind[:, :, None] == jnp.arange(kind_total, dtype=jnp.int32))
        & active_far_links[:, :, None]
    ).astype(jnp.float32)
    pressure = incident
    residual = jnp.zeros_like(incident)
    for iteration in range(ITERS):
        window = padded(pressure, (("cl", 0),), per_slab)
        surface_panels = operator_product("cew,wqk->ceqk", window_hot, window)
        direct = operator_product("cepq,ceqk->cpk", near_real, surface_panels)
        crossed = operator_product("cepq,ceqk->cpk", near_imag, surface_panels)
        returned = partner(crossed, "grp", partner_bit)
        multipole_series = operator_product("cqp,cpk->cqk", to_moments, pressure)
        moment_values = operator_product("ym,ysw->msw", box_onehot_matrix, multipole_series)
        shard_piece = lax.all_gather(moment_values, "cl", axis=0, tiled=True)
        length_total = shard_piece.shape[0]
        source_hot = (
            far_source[:, :, None] == jnp.arange(length_total, dtype=jnp.int32)[None, None, :]
        ).astype(jnp.float32)
        weights = operator_product("tfj,tfy->tjy", source_hot, kind_hot)
        grouped = operator_product("tjy,jqk->tyqk", weights, shard_piece)
        local_field = operator_product("yrq,tyqk->trk", transfer_ops, grouped)
        cluster_local = operator_product("cb,brk->crk", box_onehot_matrix, local_field)
        applied = (
            pressure
            + (direct + parity * returned)
            + operator_product("cpr,crk->cpk", from_locals, cluster_local)
        )
        residual = incident - applied
        pressure = pressure + DAMPING * residual
    return (pressure, residual)


F32, BF16 = jnp.float32, jnp.bfloat16
MESH = pl.DeviceIdType.MESH


def halves(x):
    high = x.astype(BF16)
    return high, (x - high.astype(F32)).astype(BF16)


def stacked(x):
    return jnp.concatenate(halves(x), axis=0)


def product(left, right):
    return jnp.dot(left, right, preferred_element_type=F32)


def product_nt(left, right):
    return lax.dot_general(left, right, (((1,), (1,)), ((), ())), preferred_element_type=F32)


def fold(o):
    m, n = o.shape[0] // 2, o.shape[1] // 2
    return o[:m, :n] + (o[:m, n:] + o[m:, :n])


def body(
    incident,
    near_real,
    near_imag,
    to_moments,
    from_locals,
    transfer_ops,
    near_index,
    near_count,
    cluster_box,
    far_source,
    far_kind,
    far_count,
    held_out,
    applied_out,
    near_raw,
    ops_raw,
    inc,
    maps_raw,
    near_rows,
    panels,
    ops_hl,
    maps_hl,
    hot,
    grouped,
    info,
    info_all,
    turned_inc,
    iterate,
    window,
    window_hl,
    send_out,
    recv_out,
    send_home,
    recv_home,
    moved,
    swapped,
    load_sem,
    sems,
):
    n, grps = lax.axis_size("cl"), lax.axis_size("grp")
    me, grp = lax.axis_index("cl"), lax.axis_index("grp")
    clusters, points, width = incident.shape
    boxes, far_max = far_source.shape
    near_max = near_index.shape[1]
    kinds, coeffs = transfer_ops.shape[0], transfer_ops.shape[1]
    share, half = width // n, width // 2
    piece = share // 2
    part = grp // (grps // 2)
    low = lax.rem(grp, grps // 2)
    other = lax.rem(grp + grps // 2, grps)
    after, before = lax.rem(me + 1, n), lax.rem(me + n - 1, n)
    mine, theirs = pl.ds(part * half, half), pl.ds((1 - part) * half, half)

    barrier = pltpu.get_barrier_semaphore()
    for j in range(n):
        peer = lax.rem(me + j, n)
        if j:
            pl.semaphore_signal(barrier, inc=1, device_id={"cl": peer}, device_id_type=MESH)
        pl.semaphore_signal(barrier, inc=1, device_id={"cl": peer, "grp": other}, device_id_type=MESH)

    loads = [
        pltpu.make_async_copy(incident, inc, load_sem.at[0]),
        pltpu.make_async_copy(to_moments, maps_raw.at[0], load_sem.at[1]),
        pltpu.make_async_copy(from_locals, maps_raw.at[1], load_sem.at[2]),
        pltpu.make_async_copy(transfer_ops, ops_raw, load_sem.at[3]),
        pltpu.make_async_copy(near_real, near_raw.at[0], load_sem.at[4]),
        pltpu.make_async_copy(near_imag, near_raw.at[1], load_sem.at[5]),
    ]
    for load in loads:
        load.start()

    sent = []

    def remote(source, target, kind, j, device):
        copy = pltpu.make_async_remote_copy(
            src_ref=source,
            dst_ref=target,
            send_sem=sems.at[0, kind, j],
            recv_sem=sems.at[1, kind, j],
            device_id=device,
            device_id_type=MESH,
        )
        copy.start()
        sent.append(copy)
        return copy

    far_first = sorted(range(n), key=lambda j: -min(j, n - j))

    def moments(fields):
        parts = [
            fold(product_nt(stacked(fields[c]), maps_hl[0, c])) for c in range(clusters)
        ]
        totals = []
        for b in range(boxes):
            total = jnp.zeros((width, coeffs), F32)
            for c in range(clusters):
                total = total + jnp.where(cluster_box[c] == b, 1.0, 0.0).astype(F32) * parts[c]
            totals.append(total)
        return totals

    info[...] = jnp.full(info.shape, -1, jnp.int32)
    lane = lax.broadcasted_iota(jnp.int32, (1, far_max), 1)
    for b in range(boxes):
        info[b : b + 1, 0:far_max] = far_source[b : b + 1, :]
        info[boxes + b : boxes + b + 1, 0:far_max] = jnp.where(
            lane < far_count[b], far_kind[b : b + 1, :], -1
        )
    info_all[me] = info[...]

    loads[0].wait()
    for c in range(clusters):
        turned_inc[c] = inc[c].T
    window[0, clusters : 2 * clusters, mine, :] = turned_inc[:, mine, :]
    loads[1].wait()
    for c in range(clusters):
        maps_hl[0, c] = stacked(maps_raw[0, c])
    totals = moments([turned_inc[c] for c in range(clusters)])
    for b in range(boxes):
        for side in range(2):
            for d in range(n):
                at = side * half + d * piece
                send_out[0, d, b, side * piece : (side + 1) * piece, :] = totals[b][at : at + piece]
    own = pl.ds(part * piece, piece)
    recv_out[0, me, :, own, :] = send_out[0, me, :, own, :]

    pl.semaphore_wait(barrier, 2 * n - 1)
    info_copies = [
        remote(info, info_all.at[me], 0, j, {"cl": lax.rem(me + j, n)}) for j in range(1, n)
    ]
    out_copies = []
    across = pl.ds((1 - part) * piece, piece)
    for j in far_first:
        peer = lax.rem(me + j, n)
        out_copies.append(
            remote(
                send_out.at[0, peer, :, across, :],
                recv_out.at[0, me, :, own, :],
                1,
                n + j,
                {"cl": peer, "grp": other},
            )
        )
        if j:
            out_copies.append(
                remote(
                    send_out.at[0, peer, :, own, :],
                    recv_out.at[0, me, :, own, :],
                    1,
                    j,
                    {"cl": peer},
                )
            )
    window_copies = []
    for at, (slot, peer) in enumerate(((0, after), (2, before), (1, me))):
        rows = pl.ds(slot * clusters, clusters)
        window_copies.append(
            remote(
                turned_inc.at[:, theirs, :],
                window.at[0, rows, mine, :],
                2,
                at,
                {"cl": peer, "grp": other},
            )
        )
        if slot != 1:
            window_copies.append(
                remote(
                    turned_inc.at[:, mine, :], window.at[0, rows, mine, :], 2, 3 + at, {"cl": peer}
                )
            )

    loads[3].wait()

    @pl.loop(0, kinds)
    def _(kind):
        turned = ops_raw[kind].T
        high, lower = halves(turned)
        ops_hl[kind, :, 0:coeffs] = high
        ops_hl[kind, :, coeffs : 2 * coeffs] = lower

    for copy in info_copies:
        copy.wait_recv()
    rows = n * boxes * share
    kind_id = lax.broadcasted_iota(jnp.int32, (kinds, info.shape[1]), 0)
    source_id = lax.broadcasted_iota(jnp.int32, (rows, info.shape[1]), 0) // share
    same = (
        lax.broadcasted_iota(jnp.int32, (share, rows), 1) % share
        == lax.broadcasted_iota(jnp.int32, (share, rows), 0)
    )
    same = jnp.where(same, 1.0, 0.0).astype(F32)
    for d in range(n):
        for b in range(boxes):
            of_kind = jnp.where(info_all[d, boxes + b : boxes + b + 1, :] == kind_id, 1.0, 0.0)
            of_source = jnp.where(info_all[d, b : b + 1, :] == source_id, 1.0, 0.0)
            weight = product_nt(of_kind.astype(BF16), of_source.astype(BF16))
            spread = weight[:, None, :] * same[None, :, :]
            at = (d * boxes + b) * share
            hot[:, at : at + share, :] = spread.astype(BF16)
    loads[2].wait()
    for c in range(clusters):
        maps_hl[1, c] = stacked(maps_raw[1, c])
    loads[4].wait()
    loads[5].wait()
    for kind in range(2):
        for c in range(clusters):
            for e in range(near_max):
                live = jnp.where(e < near_count[c], 1.0, 0.0).astype(F32)
                high, lower = halves(near_raw[kind, c, e] * live)
                cols = slice(e * points, (e + 1) * points)
                near_rows[c, kind * points : (kind + 1) * points, cols] = high
                near_rows[c, (2 + kind) * points : (3 + kind) * points, cols] = lower

    def translate(sweep):
        series_hl = jnp.concatenate(halves(recv_out[sweep].reshape(rows, coeffs)), axis=1)
        for kind in range(kinds):
            both = product(hot[kind], series_hl)
            high, lower = halves(both[:, :coeffs] + both[:, coeffs:])
            cols = slice(kind * coeffs, (kind + 1) * coeffs)
            grouped[0:rows, cols] = high
            grouped[rows : 2 * rows, cols] = lower
        local = fold(product(grouped[...], ops_hl[...].reshape(kinds * coeffs, 2 * coeffs)))
        send_home[sweep] = local.reshape(n, boxes, share, coeffs)

    def near(sweep):
        for w in range(3 * clusters):
            window_hl[w] = stacked(window[sweep, w])
        found = []
        for c in range(clusters):
            for e in range(near_max):
                panels[c, :, e * points : (e + 1) * points] = window_hl[near_index[c, e]]
            o = fold(product_nt(panels[c], near_rows[c]))
            crossed = o[:, points:]
            found.append(
                o[:, :points] + jnp.concatenate([-crossed[half:], crossed[:half]], axis=0)
            )
        return found

    def chosen(fields, c):
        field = jnp.zeros((width, coeffs), F32)
        for b in range(boxes):
            field = field + jnp.where(cluster_box[c] == b, 1.0, 0.0).astype(F32) * fields[b]
        return stacked(field)

    for copy in out_copies:
        copy.wait_recv()
    translate(0)
    recv_home[0, me] = send_home[0, me]
    home_copies = []
    for j in far_first[:-1]:
        peer = lax.rem(me + j, n)
        home_copies.append(
            remote(send_home.at[0, peer], recv_home.at[0, me], 3, j, {"cl": peer})
        )
    for copy in window_copies:
        copy.wait_recv()
    direct = near(0)
    for copy in home_copies:
        copy.wait_recv()
    fields = [
        jnp.concatenate(
            [
                recv_home[0, d, b, side * piece : (side + 1) * piece, :]
                for side in range(2)
                for d in range(n)
            ],
            axis=0,
        )
        for b in range(boxes)
    ]
    for c in range(clusters):
        held = window[0, clusters + c]
        far = fold(product_nt(chosen(fields, c), maps_hl[1, c]))
        applied = held + direct[c] + far
        iterate[c] = held + DAMPING * (held - applied)

    totals = moments([iterate[c] for c in range(clusters)])
    for b in range(boxes):
        for side in range(2):
            for d in range(n):
                at = side * half + d * piece
                send_out[1, d, b, side * piece : (side + 1) * piece, :] = totals[b][at : at + piece]
    recv_out[1, me] = send_out[1, me]
    out_copies = []
    for j in far_first[:-1]:
        peer = lax.rem(me + j, n)
        out_copies.append(remote(send_out.at[1, peer], recv_out.at[1, me], 4, j, {"cl": peer}))
    window_copies = [
        remote(iterate, window.at[1, pl.ds(0, clusters)], 5, 0, {"cl": after}),
        remote(iterate, window.at[1, pl.ds(2 * clusters, clusters)], 5, 1, {"cl": before}),
    ]
    window[1, clusters : 2 * clusters] = iterate[...]
    held_copy = remote(
        iterate.at[:, theirs, :], swapped.at[0, :, mine, :], 6, 0, {"grp": other}
    )
    swapped[0, :, mine, :] = iterate[:, mine, :]
    for copy in out_copies:
        copy.wait_recv()
    translate(1)
    recv_home[1, me, :, own, :] = send_home[1, me, :, own, :]
    home_copies = []
    for j in far_first:
        peer = lax.rem(me + j, n)
        home_copies.append(
            remote(
                send_home.at[1, peer, :, across, :],
                recv_home.at[1, me, :, own, :],
                7,
                n + j,
                {"cl": peer, "grp": other},
            )
        )
        if j:
            home_copies.append(
                remote(
                    send_home.at[1, peer, :, own, :],
                    recv_home.at[1, me, :, own, :],
                    7,
                    j,
                    {"cl": peer},
                )
            )
    for copy in window_copies:
        copy.wait_recv()
    direct = near(1)
    for c in range(clusters):
        moved[c] = iterate[c] + direct[c]
    moved_copy = remote(moved.at[:, theirs, :], swapped.at[1, :, mine, :], 6, 1, {"grp": other})
    swapped[1, :, mine, :] = moved[:, mine, :]
    held_copy.wait_recv()
    for c in range(clusters):
        held_out[c] = swapped[0, c].T
    moved_copy.wait_recv()
    near_part = [swapped[1, c].T for c in range(clusters)]
    for copy in home_copies:
        copy.wait_recv()
    fields = [
        jnp.concatenate(
            [
                recv_home[1, d, b, side * piece : (side + 1) * piece, :]
                for side in range(2)
                for d in range(n)
            ],
            axis=0,
        )
        for b in range(boxes)
    ]
    for c in range(clusters):
        applied_out[c] = near_part[c] + fold(product_nt(maps_hl[1, c], chosen(fields, c)))

    for copy in sent:
        copy.wait_send()


def sweeps(*args):
    incident, near_real, transfer_ops, far_source = args[0], args[1], args[5], args[9]
    n, grps = lax.axis_size("cl"), lax.axis_size("grp")
    clusters, points, width = incident.shape
    near_max = near_real.shape[1]
    kinds, coeffs = transfer_ops.shape[:2]
    boxes, far_max = far_source.shape
    share = width // n
    tiled = width % n == 0 and share % 16 == 0 and far_max <= 128 and 2 * boxes <= 8
    tiled = tiled and grps % 2 == 0 and n >= 3
    if not (tiled and ITERS == 2 and points % 128 == 0 and coeffs % 128 == 0 and width % 128 == 0):
        return shards(*args)
    rows = n * boxes * share
    vmem, smem, hbm = (
        pl.BlockSpec(memory_space=space) for space in (pltpu.VMEM, pltpu.SMEM, pl.ANY)
    )
    field = jax.ShapeDtypeStruct(incident.shape, F32)
    turned = (clusters, width, points)
    exchanged = pltpu.VMEM((ITERS, n, boxes, share, coeffs), F32)
    held, applied = (
        pl.pallas_call(
            body,
            out_shape=(field, field),
            in_specs=[hbm, hbm, hbm, hbm, hbm, hbm, smem, smem, smem, vmem, vmem, smem],
            out_specs=(vmem, vmem),
            scratch_shapes=[
                pltpu.VMEM((2,) + near_real.shape, F32),
                pltpu.VMEM(transfer_ops.shape, F32),
                pltpu.VMEM(incident.shape, F32),
                pltpu.VMEM((2, clusters, coeffs, points), F32),
                pltpu.VMEM((clusters, 4 * points, near_max * points), BF16),
                pltpu.VMEM((clusters, 2 * width, near_max * points), BF16),
                pltpu.VMEM((kinds, coeffs, 2 * coeffs), BF16),
                pltpu.VMEM((2, clusters, 2 * coeffs, points), BF16),
                pltpu.VMEM((kinds, rows, rows), BF16),
                pltpu.VMEM((2 * rows, kinds * coeffs), BF16),
                pltpu.VMEM((8, 128), jnp.int32),
                pltpu.VMEM((n, 8, 128), jnp.int32),
                pltpu.VMEM(turned, F32),
                pltpu.VMEM(turned, F32),
                pltpu.VMEM((ITERS, 3 * clusters, width, points), F32),
                pltpu.VMEM((3 * clusters, 2 * width, points), BF16),
                exchanged,
                exchanged,
                exchanged,
                exchanged,
                pltpu.VMEM(turned, F32),
                pltpu.VMEM((2,) + turned, F32),
                pltpu.SemaphoreType.DMA((6,)),
                pltpu.SemaphoreType.DMA((2, 8, max(2 * n, 6))),
            ],
            compiler_params=pltpu.CompilerParams(
                collective_id=0, has_side_effects=True, vmem_limit_bytes=60 * 1024 * 1024
            ),
        )(*args)
    )
    residual = incident - applied
    return (held + DAMPING * residual, residual)


def solution(mesh):
    return jax.shard_map(
        sweeps,
        mesh=mesh,
        in_specs=(
            P("cl", None, "grp"),
            P("cl", None, None, None),
            P("cl", None, None, None),
            P("cl", None, None),
            P("cl", None, None),
            P(),
            P("cl", None),
            P("cl"),
            P("cl"),
            P("cl", None),
            P("cl", None),
            P("cl"),
        ),
        out_specs=(P("cl", None, "grp"), P("cl", None, "grp")),
        check_vma=False,
    )
```

```python
import functools

import jax
import jax.numpy as jnp
from jax import lax
from jax.experimental import pallas as pl
from jax.experimental.pallas import tpu as pltpu
from jax.sharding import PartitionSpec as P

ITERS = 2


DAMPING = 0.7


def padded(block, sides, width):
    for axis, dim in sides:
        count = lax.axis_size(axis)
        forward = [(i, i + 1) for i in range(count - 1)]
        forward.append((count - 1, 0))
        backward = [(target, source) for source, target in forward]
        low = lax.ppermute(
            lax.slice_in_dim(block, block.shape[dim] - width, None, axis=dim), axis, forward
        )
        high = lax.ppermute(lax.slice_in_dim(block, 0, width, axis=dim), axis, backward)
        block = jnp.concatenate([low, block, high], axis=dim)
    return block


def partner(x, axis, bit):
    return lax.ppermute(x, axis, [(i, i ^ 1 << bit) for i in range(lax.axis_size(axis))])


def operator_product(form, left, right):
    return jnp.einsum(form, left, right, precision=lax.Precision.HIGHEST)


def shards(
    incident,
    near_real,
    near_imag,
    to_moments,
    from_locals,
    transfer_ops,
    near_index,
    near_count,
    cluster_box,
    far_source,
    far_kind,
    far_count,
):
    per_slab, points, width = incident.shape
    box_count, far_max = far_source.shape
    kind_total, coeffs = (transfer_ops.shape[0], transfer_ops.shape[1])
    near_max = near_index.shape[1]
    parity = jnp.where(lax.axis_index("grp") < lax.axis_size("grp") // 2, -1.0, 1.0).astype(
        jnp.float32
    )
    partner_bit = lax.axis_size("grp").bit_length() - 2
    live_near = (jnp.arange(near_max, dtype=jnp.int32)[None, :] < near_count[:, None]).astype(
        jnp.float32
    )
    window_hot = (
        near_index[:, :, None] == jnp.arange(3 * per_slab, dtype=jnp.int32)
    ).astype(jnp.float32) * live_near[:, :, None]
    box_onehot_matrix = (
        cluster_box[:, None] == jnp.arange(box_count, dtype=jnp.int32)[None, :]
    ).astype(jnp.float32)
    active_far_links = jnp.arange(far_max, dtype=jnp.int32)[None, :] < far_count[:, None]
    kind_hot = (
        (far_kind[:, :, None] == jnp.arange(kind_total, dtype=jnp.int32))
        & active_far_links[:, :, None]
    ).astype(jnp.float32)
    pressure = incident
    residual = jnp.zeros_like(incident)
    for iteration in range(ITERS):
        window = padded(pressure, (("cl", 0),), per_slab)
        surface_panels = operator_product("cew,wqk->ceqk", window_hot, window)
        direct = operator_product("cepq,ceqk->cpk", near_real, surface_panels)
        crossed = operator_product("cepq,ceqk->cpk", near_imag, surface_panels)
        returned = partner(crossed, "grp", partner_bit)
        multipole_series = operator_product("cqp,cpk->cqk", to_moments, pressure)
        moment_values = operator_product("ym,ysw->msw", box_onehot_matrix, multipole_series)
        shard_piece = lax.all_gather(moment_values, "cl", axis=0, tiled=True)
        length_total = shard_piece.shape[0]
        source_hot = (
            far_source[:, :, None] == jnp.arange(length_total, dtype=jnp.int32)[None, None, :]
        ).astype(jnp.float32)
        weights = operator_product("tfj,tfy->tjy", source_hot, kind_hot)
        grouped = operator_product("tjy,jqk->tyqk", weights, shard_piece)
        local_field = operator_product("yrq,tyqk->trk", transfer_ops, grouped)
        cluster_local = operator_product("cb,brk->crk", box_onehot_matrix, local_field)
        applied = (
            pressure
            + (direct + parity * returned)
            + operator_product("cpr,crk->cpk", from_locals, cluster_local)
        )
        residual = incident - applied
        pressure = pressure + DAMPING * residual
    return (pressure, residual)


F32, BF16 = jnp.float32, jnp.bfloat16
MESH = pl.DeviceIdType.MESH


def halves(x):
    high = x.astype(BF16)
    return high, (x - high.astype(F32)).astype(BF16)


def product(left, right):
    return jnp.dot(left, right, preferred_element_type=F32)


def fold(o):
    m, n = o.shape[0] // 2, o.shape[1] // 2
    return o[:m, :n] + (o[:m, n:] + o[m:, :n])


def body(
    incident,
    near_real,
    near_imag,
    to_moments,
    from_locals,
    transfer_ops,
    near_index,
    near_count,
    cluster_box,
    far_source,
    far_kind,
    far_count,
    held_out,
    applied_out,
    near_raw,
    ops_raw,
    near_rows,
    panels,
    ops_hl,
    hot,
    grouped,
    info,
    info_all,
    iterate,
    window,
    window_hl,
    send_out,
    recv_out,
    send_home,
    recv_home,
    crossed,
    returned,
    load_sem,
    sems,
):
    n, grps = lax.axis_size("cl"), lax.axis_size("grp")
    me, grp = lax.axis_index("cl"), lax.axis_index("grp")
    clusters, points, width = incident.shape
    boxes, far_max = far_source.shape
    near_max = near_index.shape[1]
    kinds, coeffs = transfer_ops.shape[0], transfer_ops.shape[1]
    share = width // n
    other = lax.rem(grp + grps // 2, grps)
    parity = jnp.where(grp < grps // 2, -1.0, 1.0).astype(F32)
    after, before = lax.rem(me + 1, n), lax.rem(me + n - 1, n)

    barrier = pltpu.get_barrier_semaphore()
    for j in range(1, n):
        pl.semaphore_signal(barrier, inc=1, device_id={"cl": lax.rem(me + j, n)}, device_id_type=MESH)
    pl.semaphore_signal(barrier, inc=1, device_id={"grp": other}, device_id_type=MESH)

    loads = [
        pltpu.make_async_copy(transfer_ops, ops_raw, load_sem.at[0]),
        pltpu.make_async_copy(near_real, near_raw.at[0], load_sem.at[1]),
        pltpu.make_async_copy(near_imag, near_raw.at[1], load_sem.at[2]),
    ]
    for load in loads:
        load.start()

    sent = []

    def remote(source, target, kind, j, device):
        copy = pltpu.make_async_remote_copy(
            src_ref=source,
            dst_ref=target,
            send_sem=sems.at[0, kind, j],
            recv_sem=sems.at[1, kind, j],
            device_id=device,
            device_id_type=MESH,
        )
        copy.start()
        sent.append(copy)
        return copy

    def exchange(source, target, kind):
        copies = []
        for j in sorted(range(1, n), key=lambda j: -min(j, n - j)):
            peer = lax.rem(me + j, n)
            copies.append(remote(source.at[peer], target.at[me], kind, j, {"cl": peer}))
        return copies

    def moments(current, sweep):
        parts = []
        for c in range(clusters):
            left = jnp.concatenate(halves(to_moments[c]), axis=0)
            right = jnp.concatenate(halves(current[c]), axis=1)
            parts.append(fold(product(left, right)).T)
        for b in range(boxes):
            total = jnp.zeros((width, coeffs), F32)
            for c in range(clusters):
                total = total + jnp.where(cluster_box[c] == b, 1.0, 0.0).astype(F32) * parts[c]
            for d in range(n):
                send_out[sweep, d, b * share : (b + 1) * share, :] = total[d * share : (d + 1) * share, :]

    info[...] = jnp.full(info.shape, -1, jnp.int32)
    lane = lax.broadcasted_iota(jnp.int32, (1, far_max), 1)
    for b in range(boxes):
        info[b : b + 1, 0:far_max] = far_source[b : b + 1, :]
        info[boxes + b : boxes + b + 1, 0:far_max] = jnp.where(
            lane < far_count[b], far_kind[b : b + 1, :], -1
        )
    info_all[me] = info[...]
    moments(incident, 0)
    recv_out[0, me] = send_out[0, me]

    pl.semaphore_wait(barrier, n)
    info_copies = [
        remote(info, info_all.at[me], 0, j, {"cl": lax.rem(me + j, n)}) for j in range(1, n)
    ]

    for sweep in range(ITERS):
        current = incident if sweep == 0 else iterate
        base = 1 + sweep * 4
        out_copies = exchange(send_out.at[sweep], recv_out.at[sweep], base)
        slab = window.at[sweep]
        window_copies = [
            remote(current, slab.at[pl.ds(0, clusters)], base + 1, 0, {"cl": after}),
            remote(current, slab.at[pl.ds(2 * clusters, clusters)], base + 1, 1, {"cl": before}),
        ]
        if sweep == 0:
            loads[0].wait()

            @pl.loop(0, kinds)
            def _(kind):
                turned = ops_raw[kind].T
                high, low = halves(turned)
                ops_hl[kind, :, 0:coeffs] = high
                ops_hl[kind, :, coeffs : 2 * coeffs] = low

            for copy in info_copies:
                copy.wait_recv()
            rows = n * boxes * share
            kind_id = lax.broadcasted_iota(jnp.int32, (kinds, info.shape[1]), 0)
            source_id = lax.broadcasted_iota(jnp.int32, (rows, info.shape[1]), 0) // share
            same = (
                lax.broadcasted_iota(jnp.int32, (share, rows), 1) % share
                == lax.broadcasted_iota(jnp.int32, (share, rows), 0)
            )
            same = jnp.where(same, 1.0, 0.0).astype(F32)
            for d in range(n):
                for b in range(boxes):
                    of_kind = jnp.where(info_all[d, boxes + b : boxes + b + 1, :] == kind_id, 1.0, 0.0)
                    of_source = jnp.where(info_all[d, b : b + 1, :] == source_id, 1.0, 0.0)
                    weight = lax.dot_general(
                        of_kind.astype(BF16),
                        of_source.astype(BF16),
                        (((1,), (1,)), ((), ())),
                        preferred_element_type=F32,
                    )
                    spread = weight[:, None, :] * same[None, :, :]
                    at = (d * boxes + b) * share
                    hot[:, at : at + share, :] = spread.astype(BF16)
            loads[1].wait()
            loads[2].wait()
            for part in range(2):
                for c in range(clusters):
                    for e in range(near_max):
                        live = jnp.where(e < near_count[c], 1.0, 0.0).astype(F32)
                        high, low = halves(near_raw[part, c, e] * live)
                        cols = slice(e * points, (e + 1) * points)
                        near_rows[c, part * points : (part + 1) * points, cols] = high
                        near_rows[c, (2 + part) * points : (3 + part) * points, cols] = low

        for copy in out_copies:
            copy.wait_recv()
        series = recv_out[sweep].reshape(n * boxes * share, coeffs)
        series_hl = jnp.concatenate(halves(series), axis=1)
        rows = n * boxes * share
        for kind in range(kinds):
            both = product(hot[kind], series_hl)
            high, low = halves(both[:, :coeffs] + both[:, coeffs:])
            cols = slice(kind * coeffs, (kind + 1) * coeffs)
            grouped[0:rows, cols] = high
            grouped[rows : 2 * rows, cols] = low
        local = fold(product(grouped[...], ops_hl[...].reshape(kinds * coeffs, 2 * coeffs)))
        send_home[sweep] = local.reshape(n, boxes * share, coeffs)
        recv_home[sweep, me] = send_home[sweep, me]
        home_copies = exchange(send_home.at[sweep], recv_home.at[sweep], base + 2)

        window[sweep, clusters : 2 * clusters] = current[...]
        for copy in window_copies:
            copy.wait_recv()
        for w in range(3 * clusters):
            high, low = halves(window[sweep, w])
            window_hl[w, :, 0:width] = high
            window_hl[w, :, width : 2 * width] = low
        direct = []
        for c in range(clusters):
            for e in range(near_max):
                panels[c, e * points : (e + 1) * points, :] = window_hl[near_index[c, e]]
            o = fold(product(near_rows[c], panels[c]))
            direct.append(o[0:points])
            crossed[sweep, c] = o[points : 2 * points]
        crossed_copy = remote(crossed.at[sweep], returned.at[sweep], base + 3, 0, {"grp": other})

        for copy in home_copies:
            copy.wait_recv()
        fields = [
            jnp.concatenate(
                [recv_home[sweep, d, b * share : (b + 1) * share, :] for d in range(n)], axis=0
            )
            for b in range(boxes)
        ]
        far = []
        for c in range(clusters):
            field = jnp.zeros((width, coeffs), F32)
            for b in range(boxes):
                field = field + jnp.where(cluster_box[c] == b, 1.0, 0.0).astype(F32) * fields[b]
            left = jnp.concatenate(halves(from_locals[c]), axis=0)
            right = jnp.concatenate(halves(field.T), axis=1)
            far.append(fold(product(left, right)))
        crossed_copy.wait_recv()
        for c in range(clusters):
            held = current[c]
            applied = held + (direct[c] + parity * returned[sweep, c]) + far[c]
            if sweep == ITERS - 1:
                applied_out[c] = applied
                held_out[c] = held
            else:
                iterate[c] = held + DAMPING * (incident[c] - applied)
        if sweep < ITERS - 1:
            moments(iterate, sweep + 1)
            recv_out[sweep + 1, me] = send_out[sweep + 1, me]

    for copy in sent:
        copy.wait_send()


def sweeps(*args):
    incident, near_real, transfer_ops, far_source = args[0], args[1], args[5], args[9]
    n = lax.axis_size("cl")
    clusters, points, width = incident.shape
    near_max = near_real.shape[1]
    kinds, coeffs = transfer_ops.shape[:2]
    boxes, far_max = far_source.shape
    share = width // n
    tiled = width % n == 0 and share % 16 == 0 and far_max <= 128 and 2 * boxes <= 8
    if not (tiled and ITERS == 2 and points % 128 == 0 and coeffs % 128 == 0 and width % 128 == 0):
        return shards(*args)
    rows = n * boxes * share
    vmem, smem, hbm = (
        pl.BlockSpec(memory_space=space) for space in (pltpu.VMEM, pltpu.SMEM, pl.ANY)
    )
    field = pltpu.VMEM(incident.shape, F32)
    held, applied = (
        pl.pallas_call(
            body,
            out_shape=(field, field),
            in_specs=[vmem, hbm, hbm, vmem, vmem, hbm, smem, smem, smem, vmem, vmem, smem],
            out_specs=(vmem, vmem),
            scratch_shapes=[
                pltpu.VMEM((2,) + near_real.shape, F32),
                pltpu.VMEM(transfer_ops.shape, F32),
                pltpu.VMEM((clusters, 4 * points, near_max * points), BF16),
                pltpu.VMEM((clusters, near_max * points, 2 * width), BF16),
                pltpu.VMEM((kinds, coeffs, 2 * coeffs), BF16),
                pltpu.VMEM((kinds, rows, rows), BF16),
                pltpu.VMEM((2 * rows, kinds * coeffs), BF16),
                pltpu.VMEM((8, 128), jnp.int32),
                pltpu.VMEM((n, 8, 128), jnp.int32),
                pltpu.VMEM(incident.shape, F32),
                pltpu.VMEM((ITERS, 3 * clusters, points, width), F32),
                pltpu.VMEM((3 * clusters, points, 2 * width), BF16),
                pltpu.VMEM((ITERS, n, boxes * share, coeffs), F32),
                pltpu.VMEM((ITERS, n, boxes * share, coeffs), F32),
                pltpu.VMEM((ITERS, n, boxes * share, coeffs), F32),
                pltpu.VMEM((ITERS, n, boxes * share, coeffs), F32),
                pltpu.VMEM((ITERS,) + incident.shape, F32),
                pltpu.VMEM((ITERS,) + incident.shape, F32),
                pltpu.SemaphoreType.DMA((3,)),
                pltpu.SemaphoreType.DMA((2, 1 + 4 * ITERS, n)),
            ],
            compiler_params=pltpu.CompilerParams(
                collective_id=0, has_side_effects=True, vmem_limit_bytes=60 * 1024 * 1024
            ),
        )(*args)
    )
    residual = incident - applied
    return (held + DAMPING * residual, residual)


def solution(mesh):
    return jax.shard_map(
        sweeps,
        mesh=mesh,
        in_specs=(
            P("cl", None, "grp"),
            P("cl", None, None, None),
            P("cl", None, None, None),
            P("cl", None, None),
            P("cl", None, None),
            P(),
            P("cl", None),
            P("cl"),
            P("cl"),
            P("cl", None),
            P("cl", None),
            P("cl"),
        ),
        out_specs=(P("cl", None, "grp"), P("cl", None, "grp")),
        check_vma=False,
    )
```

```python
import functools

import jax
import jax.numpy as jnp
from jax import lax
from jax.experimental import pallas as pl
from jax.experimental.pallas import tpu as pltpu
from jax.sharding import PartitionSpec as P

ITERS = 2


DAMPING = 0.7


def padded(block, sides, width):
    for axis, dim in sides:
        count = lax.axis_size(axis)
        forward = [(i, i + 1) for i in range(count - 1)]
        forward.append((count - 1, 0))
        backward = [(target, source) for source, target in forward]
        low = lax.ppermute(
            lax.slice_in_dim(block, block.shape[dim] - width, None, axis=dim), axis, forward
        )
        high = lax.ppermute(lax.slice_in_dim(block, 0, width, axis=dim), axis, backward)
        block = jnp.concatenate([low, block, high], axis=dim)
    return block


def partner(x, axis, bit):
    return lax.ppermute(x, axis, [(i, i ^ 1 << bit) for i in range(lax.axis_size(axis))])


def operator_product(form, left, right):
    return jnp.einsum(form, left, right, precision=lax.Precision.HIGHEST)


def shards(
    incident,
    near_real,
    near_imag,
    to_moments,
    from_locals,
    transfer_ops,
    near_index,
    near_count,
    cluster_box,
    far_source,
    far_kind,
    far_count,
):
    per_slab, points, width = incident.shape
    box_count, far_max = far_source.shape
    kind_total, coeffs = (transfer_ops.shape[0], transfer_ops.shape[1])
    near_max = near_index.shape[1]
    parity = jnp.where(lax.axis_index("grp") < lax.axis_size("grp") // 2, -1.0, 1.0).astype(
        jnp.float32
    )
    partner_bit = lax.axis_size("grp").bit_length() - 2
    live_near = (jnp.arange(near_max, dtype=jnp.int32)[None, :] < near_count[:, None]).astype(
        jnp.float32
    )
    window_hot = (
        near_index[:, :, None] == jnp.arange(3 * per_slab, dtype=jnp.int32)
    ).astype(jnp.float32) * live_near[:, :, None]
    box_onehot_matrix = (
        cluster_box[:, None] == jnp.arange(box_count, dtype=jnp.int32)[None, :]
    ).astype(jnp.float32)
    active_far_links = jnp.arange(far_max, dtype=jnp.int32)[None, :] < far_count[:, None]
    kind_hot = (
        (far_kind[:, :, None] == jnp.arange(kind_total, dtype=jnp.int32))
        & active_far_links[:, :, None]
    ).astype(jnp.float32)
    pressure = incident
    residual = jnp.zeros_like(incident)
    for iteration in range(ITERS):
        window = padded(pressure, (("cl", 0),), per_slab)
        surface_panels = operator_product("cew,wqk->ceqk", window_hot, window)
        direct = operator_product("cepq,ceqk->cpk", near_real, surface_panels)
        crossed = operator_product("cepq,ceqk->cpk", near_imag, surface_panels)
        returned = partner(crossed, "grp", partner_bit)
        multipole_series = operator_product("cqp,cpk->cqk", to_moments, pressure)
        moment_values = operator_product("ym,ysw->msw", box_onehot_matrix, multipole_series)
        shard_piece = lax.all_gather(moment_values, "cl", axis=0, tiled=True)
        length_total = shard_piece.shape[0]
        source_hot = (
            far_source[:, :, None] == jnp.arange(length_total, dtype=jnp.int32)[None, None, :]
        ).astype(jnp.float32)
        weights = operator_product("tfj,tfy->tjy", source_hot, kind_hot)
        grouped = operator_product("tjy,jqk->tyqk", weights, shard_piece)
        local_field = operator_product("yrq,tyqk->trk", transfer_ops, grouped)
        cluster_local = operator_product("cb,brk->crk", box_onehot_matrix, local_field)
        applied = (
            pressure
            + (direct + parity * returned)
            + operator_product("cpr,crk->cpk", from_locals, cluster_local)
        )
        residual = incident - applied
        pressure = pressure + DAMPING * residual
    return (pressure, residual)


F32, BF16 = jnp.float32, jnp.bfloat16
MESH = pl.DeviceIdType.MESH


def halves(x):
    high = x.astype(BF16)
    return high, (x - high.astype(F32)).astype(BF16)


def product(left, right):
    return jnp.dot(left, right, preferred_element_type=F32)


def fold(o):
    m, n = o.shape[0] // 2, o.shape[1] // 2
    return o[:m, :n] + (o[:m, n:] + o[m:, :n])


def body(
    incident,
    near_real,
    near_imag,
    to_moments,
    from_locals,
    transfer_ops,
    near_index,
    near_count,
    cluster_box,
    far_source,
    far_kind,
    far_count,
    held_out,
    applied_out,
    near_raw,
    ops_raw,
    near_rows,
    panels,
    ops_hl,
    hot,
    grouped,
    info,
    info_all,
    iterate,
    window,
    window_hl,
    send_out,
    recv_out,
    send_home,
    recv_home,
    crossed,
    returned,
    load_sem,
    sems,
):
    n, grps = lax.axis_size("cl"), lax.axis_size("grp")
    me, grp = lax.axis_index("cl"), lax.axis_index("grp")
    clusters, points, width = incident.shape
    boxes, far_max = far_source.shape
    near_max = near_index.shape[1]
    kinds, coeffs = transfer_ops.shape[0], transfer_ops.shape[1]
    share = width // n
    other = lax.rem(grp + grps // 2, grps)
    parity = jnp.where(grp < grps // 2, -1.0, 1.0).astype(F32)
    after, before = lax.rem(me + 1, n), lax.rem(me + n - 1, n)

    barrier = pltpu.get_barrier_semaphore()
    for j in range(1, n):
        pl.semaphore_signal(barrier, inc=1, device_id={"cl": lax.rem(me + j, n)}, device_id_type=MESH)
    pl.semaphore_signal(barrier, inc=1, device_id={"grp": other}, device_id_type=MESH)

    loads = [
        pltpu.make_async_copy(transfer_ops, ops_raw, load_sem.at[0]),
        pltpu.make_async_copy(near_real, near_raw.at[0], load_sem.at[1]),
        pltpu.make_async_copy(near_imag, near_raw.at[1], load_sem.at[2]),
    ]
    for load in loads:
        load.start()

    sent = []

    def remote(source, target, kind, j, device):
        copy = pltpu.make_async_remote_copy(
            src_ref=source,
            dst_ref=target,
            send_sem=sems.at[0, kind, j],
            recv_sem=sems.at[1, kind, j],
            device_id=device,
            device_id_type=MESH,
        )
        copy.start()
        sent.append(copy)
        return copy

    def exchange(source, target, kind):
        copies = []
        for j in sorted(range(1, n), key=lambda j: -min(j, n - j)):
            peer = lax.rem(me + j, n)
            copies.append(remote(source.at[peer], target.at[me], kind, j, {"cl": peer}))
        return copies

    def moments(current, sweep):
        parts = []
        for c in range(clusters):
            left = jnp.concatenate(halves(to_moments[c]), axis=0)
            right = jnp.concatenate(halves(current[c]), axis=1)
            parts.append(fold(product(left, right)).T)
        for b in range(boxes):
            total = jnp.zeros((width, coeffs), F32)
            for c in range(clusters):
                total = total + jnp.where(cluster_box[c] == b, 1.0, 0.0).astype(F32) * parts[c]
            for d in range(n):
                send_out[sweep, d, b * share : (b + 1) * share, :] = total[d * share : (d + 1) * share, :]

    info[...] = jnp.full(info.shape, -1, jnp.int32)
    lane = lax.broadcasted_iota(jnp.int32, (1, far_max), 1)
    for b in range(boxes):
        info[b : b + 1, 0:far_max] = far_source[b : b + 1, :]
        info[boxes + b : boxes + b + 1, 0:far_max] = jnp.where(
            lane < far_count[b], far_kind[b : b + 1, :], -1
        )
    info_all[me] = info[...]
    moments(incident, 0)
    recv_out[0, me] = send_out[0, me]

    pl.semaphore_wait(barrier, n)
    info_copies = [
        remote(info, info_all.at[me], 0, j, {"cl": lax.rem(me + j, n)}) for j in range(1, n)
    ]

    for sweep in range(ITERS):
        current = incident if sweep == 0 else iterate
        base = 1 + sweep * 4
        out_copies = exchange(send_out.at[sweep], recv_out.at[sweep], base)
        slab = window.at[sweep]
        window_copies = [
            remote(current, slab.at[pl.ds(0, clusters)], base + 1, 0, {"cl": after}),
            remote(current, slab.at[pl.ds(2 * clusters, clusters)], base + 1, 1, {"cl": before}),
        ]
        if sweep == 0:
            loads[0].wait()

            @pl.loop(0, kinds)
            def _(kind):
                turned = ops_raw[kind].T
                high, low = halves(turned)
                ops_hl[kind, :, 0:coeffs] = high
                ops_hl[kind, :, coeffs : 2 * coeffs] = low

            for copy in info_copies:
                copy.wait_recv()
            rows = n * boxes * share
            kind_id = lax.broadcasted_iota(jnp.int32, (kinds, info.shape[1]), 0)
            source_id = lax.broadcasted_iota(jnp.int32, (rows, info.shape[1]), 0) // share
            same = (
                lax.broadcasted_iota(jnp.int32, (share, rows), 1) % share
                == lax.broadcasted_iota(jnp.int32, (share, rows), 0)
            )
            same = jnp.where(same, 1.0, 0.0).astype(F32)
            for d in range(n):
                for b in range(boxes):
                    of_kind = jnp.where(info_all[d, boxes + b : boxes + b + 1, :] == kind_id, 1.0, 0.0)
                    of_source = jnp.where(info_all[d, b : b + 1, :] == source_id, 1.0, 0.0)
                    weight = lax.dot_general(
                        of_kind.astype(BF16),
                        of_source.astype(BF16),
                        (((1,), (1,)), ((), ())),
                        preferred_element_type=F32,
                    )
                    spread = weight[:, None, :] * same[None, :, :]
                    at = (d * boxes + b) * share
                    hot[:, at : at + share, :] = spread.astype(BF16)
            loads[1].wait()
            loads[2].wait()
            for part in range(2):
                for c in range(clusters):
                    for e in range(near_max):
                        live = jnp.where(e < near_count[c], 1.0, 0.0).astype(F32)
                        high, low = halves(near_raw[part, c, e] * live)
                        cols = slice(e * points, (e + 1) * points)
                        at = (2 - 2 * part) * points
                        near_rows[c, at : at + points, cols] = high
                        near_rows[c, at + points : at + 2 * points, cols] = low

        for copy in out_copies:
            copy.wait_recv()
        series = recv_out[sweep].reshape(n * boxes * share, coeffs)
        series_hl = jnp.concatenate(halves(series), axis=1)
        rows = n * boxes * share
        few, quads = rows // 2, n // 2
        side = me // quads
        home_copies = []
        for turn in range(2):
            block = 1 - side if turn == 0 else side
            first = pl.multiple_of(block * few, few)
            for kind in range(kinds):
                both = product(hot[kind, pl.ds(first, few), :], series_hl)
                high, low = halves(both[:, :coeffs] + both[:, coeffs:])
                cols = slice(kind * coeffs, (kind + 1) * coeffs)
                grouped[turn, 0:few, cols] = high
                grouped[turn, few : 2 * few, cols] = low
            local = fold(product(grouped[turn], ops_hl[...].reshape(kinds * coeffs, 2 * coeffs)))
            local = local.reshape(quads, boxes * share, coeffs)
            send_home[sweep, pl.ds(block * quads, quads)] = local
            for i in range(turn, quads):
                peer = block * quads + lax.rem(me + i, quads)
                j = (1 - turn) * quads + i
                home_copies.append(
                    remote(
                        send_home.at[sweep, peer], recv_home.at[sweep, me], base + 2, j, {"cl": peer}
                    )
                )
        recv_home[sweep, me] = send_home[sweep, me]

        for w in range(clusters):
            high, low = halves(current[w])
            window_hl[clusters + w, :, 0:width] = high
            window_hl[clusters + w, :, width : 2 * width] = low
        for copy in window_copies:
            copy.wait_recv()
        for w in list(range(clusters)) + list(range(2 * clusters, 3 * clusters)):
            high, low = halves(window[sweep, w])
            window_hl[w, :, 0:width] = high
            window_hl[w, :, width : 2 * width] = low
        direct = []
        for c in range(clusters):
            for e in range(near_max):
                panels[c, e * points : (e + 1) * points, :] = window_hl[near_index[c, e]]
            crossed[sweep, c] = fold(product(near_rows[c, 0 : 2 * points], panels[c]))
        crossed_copy = remote(crossed.at[sweep], returned.at[sweep], base + 3, 0, {"grp": other})
        for c in range(clusters):
            direct.append(fold(product(near_rows[c, 2 * points : 4 * points], panels[c])))

        for copy in home_copies:
            copy.wait_recv()
        fields = [
            jnp.concatenate(
                [recv_home[sweep, d, b * share : (b + 1) * share, :] for d in range(n)], axis=0
            )
            for b in range(boxes)
        ]
        far = []
        for c in range(clusters):
            field = jnp.zeros((width, coeffs), F32)
            for b in range(boxes):
                field = field + jnp.where(cluster_box[c] == b, 1.0, 0.0).astype(F32) * fields[b]
            left = jnp.concatenate(halves(from_locals[c]), axis=0)
            right = jnp.concatenate(halves(field.T), axis=1)
            far.append(fold(product(left, right)))
        crossed_copy.wait_recv()
        for c in range(clusters):
            held = current[c]
            applied = held + (direct[c] + parity * returned[sweep, c]) + far[c]
            if sweep == ITERS - 1:
                applied_out[c] = applied
                held_out[c] = held
            else:
                iterate[c] = held + DAMPING * (incident[c] - applied)
        if sweep < ITERS - 1:
            moments(iterate, sweep + 1)
            recv_out[sweep + 1, me] = send_out[sweep + 1, me]

    for copy in sent:
        copy.wait_send()


def sweeps(*args):
    incident, near_real, transfer_ops, far_source = args[0], args[1], args[5], args[9]
    n = lax.axis_size("cl")
    clusters, points, width = incident.shape
    near_max = near_real.shape[1]
    kinds, coeffs = transfer_ops.shape[:2]
    boxes, far_max = far_source.shape
    share = width // n
    tiled = n % 2 == 0 and width % n == 0 and share % 16 == 0 and far_max <= 128 and 2 * boxes <= 8
    if not (tiled and ITERS == 2 and points % 128 == 0 and coeffs % 128 == 0 and width % 128 == 0):
        return shards(*args)
    rows = n * boxes * share
    vmem, smem, hbm = (
        pl.BlockSpec(memory_space=space) for space in (pltpu.VMEM, pltpu.SMEM, pl.ANY)
    )
    field = pltpu.VMEM(incident.shape, F32)
    held, applied = (
        pl.pallas_call(
            body,
            out_shape=(field, field),
            in_specs=[vmem, hbm, hbm, vmem, vmem, hbm, smem, smem, smem, vmem, vmem, smem],
            out_specs=(vmem, vmem),
            scratch_shapes=[
                pltpu.VMEM((2,) + near_real.shape, F32),
                pltpu.VMEM(transfer_ops.shape, F32),
                pltpu.VMEM((clusters, 4 * points, near_max * points), BF16),
                pltpu.VMEM((clusters, near_max * points, 2 * width), BF16),
                pltpu.VMEM((kinds, coeffs, 2 * coeffs), BF16),
                pltpu.VMEM((kinds, rows, rows), BF16),
                pltpu.VMEM((2, rows, kinds * coeffs), BF16),
                pltpu.VMEM((8, 128), jnp.int32),
                pltpu.VMEM((n, 8, 128), jnp.int32),
                pltpu.VMEM(incident.shape, F32),
                pltpu.VMEM((ITERS, 3 * clusters, points, width), F32),
                pltpu.VMEM((3 * clusters, points, 2 * width), BF16),
                pltpu.VMEM((ITERS, n, boxes * share, coeffs), F32),
                pltpu.VMEM((ITERS, n, boxes * share, coeffs), F32),
                pltpu.VMEM((ITERS, n, boxes * share, coeffs), F32),
                pltpu.VMEM((ITERS, n, boxes * share, coeffs), F32),
                pltpu.VMEM((ITERS,) + incident.shape, F32),
                pltpu.VMEM((ITERS,) + incident.shape, F32),
                pltpu.SemaphoreType.DMA((3,)),
                pltpu.SemaphoreType.DMA((2, 1 + 4 * ITERS, n)),
            ],
            compiler_params=pltpu.CompilerParams(
                collective_id=0, has_side_effects=True, vmem_limit_bytes=60 * 1024 * 1024
            ),
        )(*args)
    )
    residual = incident - applied
    return (held + DAMPING * residual, residual)


def solution(mesh):
    return jax.shard_map(
        sweeps,
        mesh=mesh,
        in_specs=(
            P("cl", None, "grp"),
            P("cl", None, None, None),
            P("cl", None, None, None),
            P("cl", None, None),
            P("cl", None, None),
            P(),
            P("cl", None),
            P("cl"),
            P("cl"),
            P("cl", None),
            P("cl", None),
            P("cl"),
        ),
        out_specs=(P("cl", None, "grp"), P("cl", None, "grp")),
        check_vma=False,
    )
```

```python
import functools

import jax
import jax.numpy as jnp
from jax import lax
from jax.experimental import pallas as pl
from jax.experimental.pallas import tpu as pltpu
from jax.sharding import PartitionSpec as P

ITERS = 2


DAMPING = 0.7


def padded(block, sides, width):
    for axis, dim in sides:
        count = lax.axis_size(axis)
        forward = [(i, i + 1) for i in range(count - 1)]
        forward.append((count - 1, 0))
        backward = [(target, source) for source, target in forward]
        low = lax.ppermute(
            lax.slice_in_dim(block, block.shape[dim] - width, None, axis=dim), axis, forward
        )
        high = lax.ppermute(lax.slice_in_dim(block, 0, width, axis=dim), axis, backward)
        block = jnp.concatenate([low, block, high], axis=dim)
    return block


def partner(x, axis, bit):
    return lax.ppermute(x, axis, [(i, i ^ 1 << bit) for i in range(lax.axis_size(axis))])


def operator_product(form, left, right):
    return jnp.einsum(form, left, right, precision=lax.Precision.HIGHEST)


def shards(
    incident,
    near_real,
    near_imag,
    to_moments,
    from_locals,
    transfer_ops,
    near_index,
    near_count,
    cluster_box,
    far_source,
    far_kind,
    far_count,
):
    per_slab, points, width = incident.shape
    box_count, far_max = far_source.shape
    kind_total, coeffs = (transfer_ops.shape[0], transfer_ops.shape[1])
    near_max = near_index.shape[1]
    parity = jnp.where(lax.axis_index("grp") < lax.axis_size("grp") // 2, -1.0, 1.0).astype(
        jnp.float32
    )
    partner_bit = lax.axis_size("grp").bit_length() - 2
    live_near = (jnp.arange(near_max, dtype=jnp.int32)[None, :] < near_count[:, None]).astype(
        jnp.float32
    )
    window_hot = (
        near_index[:, :, None] == jnp.arange(3 * per_slab, dtype=jnp.int32)
    ).astype(jnp.float32) * live_near[:, :, None]
    box_onehot_matrix = (
        cluster_box[:, None] == jnp.arange(box_count, dtype=jnp.int32)[None, :]
    ).astype(jnp.float32)
    active_far_links = jnp.arange(far_max, dtype=jnp.int32)[None, :] < far_count[:, None]
    kind_hot = (
        (far_kind[:, :, None] == jnp.arange(kind_total, dtype=jnp.int32))
        & active_far_links[:, :, None]
    ).astype(jnp.float32)
    pressure = incident
    residual = jnp.zeros_like(incident)
    for iteration in range(ITERS):
        window = padded(pressure, (("cl", 0),), per_slab)
        surface_panels = operator_product("cew,wqk->ceqk", window_hot, window)
        direct = operator_product("cepq,ceqk->cpk", near_real, surface_panels)
        crossed = operator_product("cepq,ceqk->cpk", near_imag, surface_panels)
        returned = partner(crossed, "grp", partner_bit)
        multipole_series = operator_product("cqp,cpk->cqk", to_moments, pressure)
        moment_values = operator_product("ym,ysw->msw", box_onehot_matrix, multipole_series)
        shard_piece = lax.all_gather(moment_values, "cl", axis=0, tiled=True)
        length_total = shard_piece.shape[0]
        source_hot = (
            far_source[:, :, None] == jnp.arange(length_total, dtype=jnp.int32)[None, None, :]
        ).astype(jnp.float32)
        weights = operator_product("tfj,tfy->tjy", source_hot, kind_hot)
        grouped = operator_product("tjy,jqk->tyqk", weights, shard_piece)
        local_field = operator_product("yrq,tyqk->trk", transfer_ops, grouped)
        cluster_local = operator_product("cb,brk->crk", box_onehot_matrix, local_field)
        applied = (
            pressure
            + (direct + parity * returned)
            + operator_product("cpr,crk->cpk", from_locals, cluster_local)
        )
        residual = incident - applied
        pressure = pressure + DAMPING * residual
    return (pressure, residual)


F32, BF16 = jnp.float32, jnp.bfloat16
MESH = pl.DeviceIdType.MESH


def halves(x):
    high = x.astype(BF16)
    return high, (x - high.astype(F32)).astype(BF16)


def product(left, right):
    return jnp.dot(left, right, preferred_element_type=F32)


def fold(o):
    m, n = o.shape[0] // 2, o.shape[1] // 2
    return o[:m, :n] + (o[:m, n:] + o[m:, :n])


def body(
    incident_in,
    near_real,
    near_imag,
    to_moments_in,
    from_locals_in,
    transfer_ops,
    near_index_in,
    near_count_in,
    cluster_box_in,
    far_source_in,
    far_kind_in,
    far_count_in,
    held_out,
    applied_out,
    incident,
    to_moments,
    from_locals,
    near_index,
    near_count,
    cluster_box,
    far_source,
    far_kind,
    far_count,
    near_raw,
    ops_raw,
    near_rows,
    panels,
    ops_hl,
    hot,
    grouped,
    info,
    info_all,
    iterate,
    window,
    window_hl,
    send_out,
    recv_out,
    send_home,
    recv_home,
    crossed,
    returned,
    load_sem,
    sems,
):
    n, grps = lax.axis_size("cl"), lax.axis_size("grp")
    me, grp = lax.axis_index("cl"), lax.axis_index("grp")
    clusters, points, width = incident.shape
    boxes, far_max = far_source.shape
    near_max = near_index.shape[1]
    kinds, coeffs = transfer_ops.shape[0], transfer_ops.shape[1]
    share = width // n
    other = lax.rem(grp + grps // 2, grps)
    parity = jnp.where(grp < grps // 2, -1.0, 1.0).astype(F32)
    after, before = lax.rem(me + 1, n), lax.rem(me + n - 1, n)

    barrier = pltpu.get_barrier_semaphore()
    for j in range(1, n):
        pl.semaphore_signal(barrier, inc=1, device_id={"cl": lax.rem(me + j, n)}, device_id_type=MESH)
    pl.semaphore_signal(barrier, inc=1, device_id={"grp": other}, device_id_type=MESH)

    pairs = (
        (transfer_ops, ops_raw),
        (near_real, near_raw.at[0]),
        (near_imag, near_raw.at[1]),
        (incident_in, incident),
        (to_moments_in, to_moments),
        (cluster_box_in, cluster_box),
        (far_source_in, far_source),
        (far_kind_in, far_kind),
        (far_count_in, far_count),
        (from_locals_in, from_locals),
        (near_index_in, near_index),
        (near_count_in, near_count),
    )
    loads = [
        pltpu.make_async_copy(source, target, load_sem.at[at])
        for at, (source, target) in enumerate(pairs)
    ]
    for load in loads[3:] + loads[:3]:
        load.start()

    sent = []

    def remote(source, target, kind, j, device, slot=None):
        copy = pltpu.make_async_remote_copy(
            src_ref=source,
            dst_ref=target,
            send_sem=sems.at[0, kind, j],
            recv_sem=sems.at[1, kind, j if slot is None else slot],
            device_id=device,
            device_id_type=MESH,
        )
        copy.start()
        sent.append(copy)
        return copy

    quads = n // 2
    side = me // quads

    def deliver(source, target, kind, turn):
        block = 1 - side if turn == 0 else side
        for i in range(turn, quads):
            if turn == 0:
                at = i + (1 - side) * (quads - 1 - 2 * i)
            else:
                at = lax.rem(me + i, quads)
            peer = block * quads + at
            j = (1 - turn) * quads + i
            remote(source.at[peer], target.at[me], kind, j, {"cl": peer}, me)

    def collect(target, kind):
        for j in range(1, n):
            sender = lax.rem(me + j, n)
            pltpu.make_async_remote_copy(
                src_ref=target.at[sender],
                dst_ref=target.at[sender],
                send_sem=sems.at[0, kind, j],
                recv_sem=sems.at[1, kind, sender],
                device_id={"cl": sender},
                device_id_type=MESH,
            ).wait_recv()

    def moments(current, sweep):
        parts = []
        for c in range(clusters):
            left = jnp.concatenate(halves(to_moments[c]), axis=0)
            right = jnp.concatenate(halves(current[c]), axis=1)
            parts.append(fold(product(left, right)).T)
        for b in range(boxes):
            total = jnp.zeros((width, coeffs), F32)
            for c in range(clusters):
                total = total + jnp.where(cluster_box[c] == b, 1.0, 0.0).astype(F32) * parts[c]
            for d in range(n):
                send_out[sweep, d, b * share : (b + 1) * share, :] = total[d * share : (d + 1) * share, :]

    for load in loads[3:]:
        load.wait()
    info[...] = jnp.full(info.shape, -1, jnp.int32)
    lane = lax.broadcasted_iota(jnp.int32, (1, far_max), 1)
    for b in range(boxes):
        info[b : b + 1, 0:far_max] = far_source[b : b + 1, :]
        info[boxes + b : boxes + b + 1, 0:far_max] = jnp.where(
            lane < far_count[b], far_kind[b : b + 1, :], -1
        )
    info_all[me] = info[...]
    moments(incident, 0)
    recv_out[0, me] = send_out[0, me]

    pl.semaphore_wait(barrier, n)
    info_copies = [
        remote(info, info_all.at[me], 0, j, {"cl": lax.rem(me + j, n)}) for j in range(1, n)
    ]

    for sweep in range(ITERS):
        current = incident if sweep == 0 else iterate
        base = 1 + sweep * 4
        for turn in range(2):
            deliver(send_out.at[sweep], recv_out.at[sweep], base, turn)
        slab = window.at[sweep]
        odd = lax.rem(me, 2)
        window_copies = [
            remote(
                current,
                slab.at[pl.ds(2 * clusters * place, clusters)],
                base + 1,
                place,
                {"cl": place * before + (1 - place) * after},
            )
            for place in (1 - odd, odd)
        ]
        if sweep == 0:
            loads[0].wait()

            @pl.loop(0, kinds)
            def _(kind):
                turned = ops_raw[kind].T
                high, low = halves(turned)
                ops_hl[kind, :, 0:coeffs] = high
                ops_hl[kind, :, coeffs : 2 * coeffs] = low

            loads[1].wait()
            loads[2].wait()
            for part in range(2):
                for c in range(clusters):
                    for e in range(near_max):
                        live = jnp.where(e < near_count[c], 1.0, 0.0).astype(F32)
                        high, low = halves(near_raw[part, c, e] * live)
                        cols = slice(e * points, (e + 1) * points)
                        at = (2 - 2 * part) * points
                        near_rows[c, at : at + points, cols] = high
                        near_rows[c, at + points : at + 2 * points, cols] = low
            for copy in info_copies:
                copy.wait_recv()
            rows = n * boxes * share
            kind_id = lax.broadcasted_iota(jnp.int32, (kinds, info.shape[1]), 0)
            source_id = lax.broadcasted_iota(jnp.int32, (rows, info.shape[1]), 0) // share
            same = (
                lax.broadcasted_iota(jnp.int32, (share, rows), 1) % share
                == lax.broadcasted_iota(jnp.int32, (share, rows), 0)
            )
            same = jnp.where(same, 1.0, 0.0).astype(F32)
            for d in range(n):
                for b in range(boxes):
                    of_kind = jnp.where(info_all[d, boxes + b : boxes + b + 1, :] == kind_id, 1.0, 0.0)
                    of_source = jnp.where(info_all[d, b : b + 1, :] == source_id, 1.0, 0.0)
                    weight = lax.dot_general(
                        of_kind.astype(BF16),
                        of_source.astype(BF16),
                        (((1,), (1,)), ((), ())),
                        preferred_element_type=F32,
                    )
                    spread = weight[:, None, :] * same[None, :, :]
                    at = (d * boxes + b) * share
                    hot[:, at : at + share, :] = spread.astype(BF16)

        collect(recv_out.at[sweep], base)
        series = recv_out[sweep].reshape(n * boxes * share, coeffs)
        series_hl = jnp.concatenate(halves(series), axis=1)
        rows = n * boxes * share
        few = rows // 2
        for turn in range(2):
            block = 1 - side if turn == 0 else side
            first = pl.multiple_of(block * few, few)
            for kind in range(kinds):
                both = product(hot[kind, pl.ds(first, few), :], series_hl)
                high, low = halves(both[:, :coeffs] + both[:, coeffs:])
                cols = slice(kind * coeffs, (kind + 1) * coeffs)
                grouped[turn, 0:few, cols] = high
                grouped[turn, few : 2 * few, cols] = low
            local = fold(product(grouped[turn], ops_hl[...].reshape(kinds * coeffs, 2 * coeffs)))
            local = local.reshape(quads, boxes * share, coeffs)
            send_home[sweep, pl.ds(block * quads, quads)] = local
            deliver(send_home.at[sweep], recv_home.at[sweep], base + 2, turn)
        recv_home[sweep, me] = send_home[sweep, me]

        for w in range(clusters):
            high, low = halves(current[w])
            window_hl[clusters + w, :, 0:width] = high
            window_hl[clusters + w, :, width : 2 * width] = low
        for copy in window_copies:
            copy.wait_recv()
        for w in list(range(clusters)) + list(range(2 * clusters, 3 * clusters)):
            high, low = halves(window[sweep, w])
            window_hl[w, :, 0:width] = high
            window_hl[w, :, width : 2 * width] = low
        direct = []
        for c in range(clusters):
            for e in range(near_max):
                panels[c, e * points : (e + 1) * points, :] = window_hl[near_index[c, e]]
            crossed[sweep, c] = fold(product(near_rows[c, 0 : 2 * points], panels[c]))
        crossed_copy = remote(crossed.at[sweep], returned.at[sweep], base + 3, 0, {"grp": other})
        for c in range(clusters):
            direct.append(fold(product(near_rows[c, 2 * points : 4 * points], panels[c])))

        collect(recv_home.at[sweep], base + 2)
        fields = [
            jnp.concatenate(
                [recv_home[sweep, d, b * share : (b + 1) * share, :] for d in range(n)], axis=0
            )
            for b in range(boxes)
        ]
        far = []
        for c in range(clusters):
            field = jnp.zeros((width, coeffs), F32)
            for b in range(boxes):
                field = field + jnp.where(cluster_box[c] == b, 1.0, 0.0).astype(F32) * fields[b]
            left = jnp.concatenate(halves(from_locals[c]), axis=0)
            right = jnp.concatenate(halves(field.T), axis=1)
            far.append(fold(product(left, right)))
        crossed_copy.wait_recv()
        for c in range(clusters):
            held = current[c]
            applied = held + (direct[c] + parity * returned[sweep, c]) + far[c]
            if sweep == ITERS - 1:
                applied_out[c] = applied
                held_out[c] = held
            else:
                iterate[c] = held + DAMPING * (incident[c] - applied)
        if sweep < ITERS - 1:
            moments(iterate, sweep + 1)
            recv_out[sweep + 1, me] = send_out[sweep + 1, me]

    for copy in sent:
        copy.wait_send()


def sweeps(*args):
    incident, near_real, transfer_ops, far_source = args[0], args[1], args[5], args[9]
    n = lax.axis_size("cl")
    clusters, points, width = incident.shape
    near_max = near_real.shape[1]
    kinds, coeffs = transfer_ops.shape[:2]
    boxes, far_max = far_source.shape
    share = width // n
    tiled = n % 2 == 0 and width % n == 0 and share % 16 == 0 and far_max <= 128 and 2 * boxes <= 8
    if not (tiled and ITERS == 2 and points % 128 == 0 and coeffs % 128 == 0 and width % 128 == 0):
        return shards(*args)
    rows = n * boxes * share
    vmem, hbm = (pl.BlockSpec(memory_space=space) for space in (pltpu.VMEM, pl.ANY))
    field = pltpu.VMEM(incident.shape, F32)
    held, applied = (
        pl.pallas_call(
            body,
            out_shape=(field, field),
            in_specs=[hbm] * 12,
            out_specs=(vmem, vmem),
            scratch_shapes=[
                pltpu.VMEM(incident.shape, F32),
                pltpu.VMEM(args[3].shape, F32),
                pltpu.VMEM(args[4].shape, F32),
                pltpu.SMEM(args[6].shape, jnp.int32),
                pltpu.SMEM(args[7].shape, jnp.int32),
                pltpu.SMEM(args[8].shape, jnp.int32),
                pltpu.VMEM(far_source.shape, jnp.int32),
                pltpu.VMEM(far_source.shape, jnp.int32),
                pltpu.SMEM(args[11].shape, jnp.int32),
                pltpu.VMEM((2,) + near_real.shape, F32),
                pltpu.VMEM(transfer_ops.shape, F32),
                pltpu.VMEM((clusters, 4 * points, near_max * points), BF16),
                pltpu.VMEM((clusters, near_max * points, 2 * width), BF16),
                pltpu.VMEM((kinds, coeffs, 2 * coeffs), BF16),
                pltpu.VMEM((kinds, rows, rows), BF16),
                pltpu.VMEM((2, rows, kinds * coeffs), BF16),
                pltpu.VMEM((8, 128), jnp.int32),
                pltpu.VMEM((n, 8, 128), jnp.int32),
                pltpu.VMEM(incident.shape, F32),
                pltpu.VMEM((ITERS, 3 * clusters, points, width), F32),
                pltpu.VMEM((3 * clusters, points, 2 * width), BF16),
                pltpu.VMEM((ITERS, n, boxes * share, coeffs), F32),
                pltpu.VMEM((ITERS, n, boxes * share, coeffs), F32),
                pltpu.VMEM((ITERS, n, boxes * share, coeffs), F32),
                pltpu.VMEM((ITERS, n, boxes * share, coeffs), F32),
                pltpu.VMEM((ITERS,) + incident.shape, F32),
                pltpu.VMEM((ITERS,) + incident.shape, F32),
                pltpu.SemaphoreType.DMA((12,)),
                pltpu.SemaphoreType.DMA((2, 1 + 4 * ITERS, n)),
            ],
            compiler_params=pltpu.CompilerParams(
                collective_id=0, has_side_effects=True, vmem_limit_bytes=60 * 1024 * 1024
            ),
        )(*args)
    )
    residual = incident - applied
    return (held + DAMPING * residual, residual)


def solution(mesh):
    return jax.shard_map(
        sweeps,
        mesh=mesh,
        in_specs=(
            P("cl", None, "grp"),
            P("cl", None, None, None),
            P("cl", None, None, None),
            P("cl", None, None),
            P("cl", None, None),
            P(),
            P("cl", None),
            P("cl"),
            P("cl"),
            P("cl", None),
            P("cl", None),
            P("cl"),
        ),
        out_specs=(P("cl", None, "grp"), P("cl", None, "grp")),
        check_vma=False,
    )
```

```python
import functools

import jax
import jax.numpy as jnp
from jax import lax
from jax.experimental import pallas as pl
from jax.experimental.pallas import tpu as pltpu
from jax.sharding import PartitionSpec as P

ITERS = 2


DAMPING = 0.7


def padded(block, sides, width):
    for axis, dim in sides:
        count = lax.axis_size(axis)
        forward = [(i, i + 1) for i in range(count - 1)]
        forward.append((count - 1, 0))
        backward = [(target, source) for source, target in forward]
        low = lax.ppermute(
            lax.slice_in_dim(block, block.shape[dim] - width, None, axis=dim), axis, forward
        )
        high = lax.ppermute(lax.slice_in_dim(block, 0, width, axis=dim), axis, backward)
        block = jnp.concatenate([low, block, high], axis=dim)
    return block


def partner(x, axis, bit):
    return lax.ppermute(x, axis, [(i, i ^ 1 << bit) for i in range(lax.axis_size(axis))])


def operator_product(form, left, right):
    return jnp.einsum(form, left, right, precision=lax.Precision.HIGHEST)


def shards(
    incident,
    near_real,
    near_imag,
    to_moments,
    from_locals,
    transfer_ops,
    near_index,
    near_count,
    cluster_box,
    far_source,
    far_kind,
    far_count,
):
    per_slab, points, width = incident.shape
    box_count, far_max = far_source.shape
    kind_total, coeffs = (transfer_ops.shape[0], transfer_ops.shape[1])
    near_max = near_index.shape[1]
    parity = jnp.where(lax.axis_index("grp") < lax.axis_size("grp") // 2, -1.0, 1.0).astype(
        jnp.float32
    )
    partner_bit = lax.axis_size("grp").bit_length() - 2
    live_near = (jnp.arange(near_max, dtype=jnp.int32)[None, :] < near_count[:, None]).astype(
        jnp.float32
    )
    window_hot = (
        near_index[:, :, None] == jnp.arange(3 * per_slab, dtype=jnp.int32)
    ).astype(jnp.float32) * live_near[:, :, None]
    box_onehot_matrix = (
        cluster_box[:, None] == jnp.arange(box_count, dtype=jnp.int32)[None, :]
    ).astype(jnp.float32)
    active_far_links = jnp.arange(far_max, dtype=jnp.int32)[None, :] < far_count[:, None]
    kind_hot = (
        (far_kind[:, :, None] == jnp.arange(kind_total, dtype=jnp.int32))
        & active_far_links[:, :, None]
    ).astype(jnp.float32)
    pressure = incident
    residual = jnp.zeros_like(incident)
    for iteration in range(ITERS):
        window = padded(pressure, (("cl", 0),), per_slab)
        surface_panels = operator_product("cew,wqk->ceqk", window_hot, window)
        direct = operator_product("cepq,ceqk->cpk", near_real, surface_panels)
        crossed = operator_product("cepq,ceqk->cpk", near_imag, surface_panels)
        returned = partner(crossed, "grp", partner_bit)
        multipole_series = operator_product("cqp,cpk->cqk", to_moments, pressure)
        moment_values = operator_product("ym,ysw->msw", box_onehot_matrix, multipole_series)
        shard_piece = lax.all_gather(moment_values, "cl", axis=0, tiled=True)
        length_total = shard_piece.shape[0]
        source_hot = (
            far_source[:, :, None] == jnp.arange(length_total, dtype=jnp.int32)[None, None, :]
        ).astype(jnp.float32)
        weights = operator_product("tfj,tfy->tjy", source_hot, kind_hot)
        grouped = operator_product("tjy,jqk->tyqk", weights, shard_piece)
        local_field = operator_product("yrq,tyqk->trk", transfer_ops, grouped)
        cluster_local = operator_product("cb,brk->crk", box_onehot_matrix, local_field)
        applied = (
            pressure
            + (direct + parity * returned)
            + operator_product("cpr,crk->cpk", from_locals, cluster_local)
        )
        residual = incident - applied
        pressure = pressure + DAMPING * residual
    return (pressure, residual)


F32, BF16 = jnp.float32, jnp.bfloat16
MESH = pl.DeviceIdType.MESH


def halves(x):
    high = x.astype(BF16)
    return high, (x - high.astype(F32)).astype(BF16)


def product(left, right):
    return jnp.dot(left, right, preferred_element_type=F32)


def fold(o):
    m, n = o.shape[0] // 2, o.shape[1] // 2
    return o[:m, :n] + (o[:m, n:] + o[m:, :n])


def body(
    incident_in,
    near_real,
    near_imag,
    to_moments_in,
    from_locals_in,
    transfer_ops,
    near_index_in,
    near_count_in,
    cluster_box_in,
    far_source_in,
    far_kind_in,
    far_count_in,
    held_out,
    applied_out,
    incident,
    to_moments,
    from_locals,
    near_index,
    near_count,
    cluster_box,
    far_source,
    far_kind,
    far_count,
    near_raw,
    ops_raw,
    near_rows,
    panels,
    ops_hl,
    hot,
    grouped,
    info,
    info_all,
    iterate,
    window,
    window_hl,
    send_out,
    recv_out,
    send_home,
    recv_home,
    crossed,
    returned,
    load_sem,
    sems,
):
    n, grps = lax.axis_size("cl"), lax.axis_size("grp")
    me, grp = lax.axis_index("cl"), lax.axis_index("grp")
    clusters, points, width = incident.shape
    boxes, far_max = far_source.shape
    near_max = near_index.shape[1]
    kinds, coeffs = transfer_ops.shape[0], transfer_ops.shape[1]
    share = width // n
    other = lax.rem(grp + grps // 2, grps)
    parity = jnp.where(grp < grps // 2, -1.0, 1.0).astype(F32)
    after, before = lax.rem(me + 1, n), lax.rem(me + n - 1, n)

    barrier = pltpu.get_barrier_semaphore()
    for j in range(1, n):
        pl.semaphore_signal(barrier, inc=1, device_id={"cl": lax.rem(me + j, n)}, device_id_type=MESH)
    pl.semaphore_signal(barrier, inc=1, device_id={"grp": other}, device_id_type=MESH)

    pairs = (
        (transfer_ops, ops_raw),
        (near_real, near_raw.at[0]),
        (near_imag, near_raw.at[1]),
        (incident_in, incident),
        (to_moments_in, to_moments),
        (cluster_box_in, cluster_box),
        (far_source_in, far_source),
        (far_kind_in, far_kind),
        (far_count_in, far_count),
        (from_locals_in, from_locals),
        (near_index_in, near_index),
        (near_count_in, near_count),
    )
    loads = [
        pltpu.make_async_copy(source, target, load_sem.at[at])
        for at, (source, target) in enumerate(pairs)
    ]
    for load in loads[3:] + loads[:3]:
        load.start()

    sent = []

    def remote(source, target, kind, j, device, slot=None):
        copy = pltpu.make_async_remote_copy(
            src_ref=source,
            dst_ref=target,
            send_sem=sems.at[0, kind, j],
            recv_sem=sems.at[1, kind, j if slot is None else slot],
            device_id=device,
            device_id_type=MESH,
        )
        copy.start()
        sent.append(copy)
        return copy

    quads = n // 2
    side = me // quads

    def deliver(source, target, kind, turn):
        block = 1 - side if turn == 0 else side
        for i in range(turn, quads):
            if turn == 0:
                at = i + (1 - side) * (quads - 1 - 2 * i)
            else:
                at = lax.rem(me + i, quads)
            peer = block * quads + at
            j = (1 - turn) * quads + i
            remote(source.at[peer], target.at[me], kind, j, {"cl": peer}, me)

    def collect(target, kind):
        for j in range(1, n):
            sender = lax.rem(me + j, n)
            pltpu.make_async_remote_copy(
                src_ref=target.at[sender],
                dst_ref=target.at[sender],
                send_sem=sems.at[0, kind, j],
                recv_sem=sems.at[1, kind, sender],
                device_id={"cl": sender},
                device_id_type=MESH,
            ).wait_recv()

    def moments(current, sweep):
        parts = []
        for c in range(clusters):
            left = jnp.concatenate(halves(to_moments[c]), axis=0)
            right = jnp.concatenate(halves(current[c]), axis=1)
            parts.append(fold(product(left, right)).T)
        for b in range(boxes):
            total = jnp.zeros((width, coeffs), F32)
            for c in range(clusters):
                total = total + jnp.where(cluster_box[c] == b, 1.0, 0.0).astype(F32) * parts[c]
            for d in range(n):
                send_out[sweep, d, b * share : (b + 1) * share, :] = total[d * share : (d + 1) * share, :]

    for load in loads[3:]:
        load.wait()
    info[...] = jnp.full(info.shape, -1, jnp.int32)
    lane = lax.broadcasted_iota(jnp.int32, (1, far_max), 1)
    for b in range(boxes):
        info[b : b + 1, 0:far_max] = far_source[b : b + 1, :]
        info[boxes + b : boxes + b + 1, 0:far_max] = jnp.where(
            lane < far_count[b], far_kind[b : b + 1, :], -1
        )
    info_all[me] = info[...]
    moments(incident, 0)
    recv_out[0, me] = send_out[0, me]

    pl.semaphore_wait(barrier, n)
    info_copies = [
        remote(info, info_all.at[me], 0, j, {"cl": lax.rem(me + j, n)}) for j in range(1, n)
    ]

    for sweep in range(ITERS):
        current = incident if sweep == 0 else iterate
        base = 1 + sweep * 4
        odd = lax.rem(me, 2)
        slab = window.at[sweep]
        window_copies = []

        def widen(place):
            window_copies.append(
                remote(
                    current,
                    slab.at[pl.ds(2 * clusters * place, clusters)],
                    base + 1,
                    place,
                    {"cl": place * before + (1 - place) * after},
                )
            )

        ahead = sweep in (1,)
        deliver(send_out.at[sweep], recv_out.at[sweep], base, 0)
        if ahead:
            widen(1 - odd)
        deliver(send_out.at[sweep], recv_out.at[sweep], base, 1)
        if not ahead:
            widen(1 - odd)
        widen(odd)
        if sweep == 0:
            loads[0].wait()

            @pl.loop(0, kinds)
            def _(kind):
                turned = ops_raw[kind].T
                high, low = halves(turned)
                ops_hl[kind, :, 0:coeffs] = high
                ops_hl[kind, :, coeffs : 2 * coeffs] = low

            loads[1].wait()
            loads[2].wait()
            for part in range(2):
                for c in range(clusters):
                    for e in range(near_max):
                        live = jnp.where(e < near_count[c], 1.0, 0.0).astype(F32)
                        high, low = halves(near_raw[part, c, e] * live)
                        cols = slice(e * points, (e + 1) * points)
                        at = (2 - 2 * part) * points
                        near_rows[c, at : at + points, cols] = high
                        near_rows[c, at + points : at + 2 * points, cols] = low
            for copy in info_copies:
                copy.wait_recv()
            rows = n * boxes * share
            kind_id = lax.broadcasted_iota(jnp.int32, (kinds, info.shape[1]), 0)
            source_id = lax.broadcasted_iota(jnp.int32, (rows, info.shape[1]), 0) // share
            same = (
                lax.broadcasted_iota(jnp.int32, (share, rows), 1) % share
                == lax.broadcasted_iota(jnp.int32, (share, rows), 0)
            )
            same = jnp.where(same, 1.0, 0.0).astype(F32)
            for d in range(n):
                for b in range(boxes):
                    of_kind = jnp.where(info_all[d, boxes + b : boxes + b + 1, :] == kind_id, 1.0, 0.0)
                    of_source = jnp.where(info_all[d, b : b + 1, :] == source_id, 1.0, 0.0)
                    weight = lax.dot_general(
                        of_kind.astype(BF16),
                        of_source.astype(BF16),
                        (((1,), (1,)), ((), ())),
                        preferred_element_type=F32,
                    )
                    spread = weight[:, None, :] * same[None, :, :]
                    at = (d * boxes + b) * share
                    hot[:, at : at + share, :] = spread.astype(BF16)

        collect(recv_out.at[sweep], base)
        series = recv_out[sweep].reshape(n * boxes * share, coeffs)
        series_hl = jnp.concatenate(halves(series), axis=1)
        rows = n * boxes * share
        few = rows // 2
        for turn in range(2):
            block = 1 - side if turn == 0 else side
            first = pl.multiple_of(block * few, few)
            for kind in range(kinds):
                both = product(hot[kind, pl.ds(first, few), :], series_hl)
                high, low = halves(both[:, :coeffs] + both[:, coeffs:])
                cols = slice(kind * coeffs, (kind + 1) * coeffs)
                grouped[turn, 0:few, cols] = high
                grouped[turn, few : 2 * few, cols] = low
            local = fold(product(grouped[turn], ops_hl[...].reshape(kinds * coeffs, 2 * coeffs)))
            local = local.reshape(quads, boxes * share, coeffs)
            send_home[sweep, pl.ds(block * quads, quads)] = local
            deliver(send_home.at[sweep], recv_home.at[sweep], base + 2, turn)
        recv_home[sweep, me] = send_home[sweep, me]

        for w in range(clusters):
            high, low = halves(current[w])
            window_hl[clusters + w, :, 0:width] = high
            window_hl[clusters + w, :, width : 2 * width] = low
        for copy in window_copies:
            copy.wait_recv()
        for w in list(range(clusters)) + list(range(2 * clusters, 3 * clusters)):
            high, low = halves(window[sweep, w])
            window_hl[w, :, 0:width] = high
            window_hl[w, :, width : 2 * width] = low
        direct, crossed_copies = [], []
        for c in range(clusters):
            for e in range(near_max):
                panels[c, e * points : (e + 1) * points, :] = window_hl[near_index[c, e]]
            crossed[sweep, c] = fold(product(near_rows[c, 0 : 2 * points], panels[c]))
            crossed_copies.append(
                remote(crossed.at[sweep, c], returned.at[sweep, c], base + 3, c, {"grp": other})
            )
        for c in range(clusters):
            direct.append(fold(product(near_rows[c, 2 * points : 4 * points], panels[c])))

        collect(recv_home.at[sweep], base + 2)
        fields = [
            jnp.concatenate(
                [recv_home[sweep, d, b * share : (b + 1) * share, :] for d in range(n)], axis=0
            )
            for b in range(boxes)
        ]
        far = []
        for c in range(clusters):
            field = jnp.zeros((width, coeffs), F32)
            for b in range(boxes):
                field = field + jnp.where(cluster_box[c] == b, 1.0, 0.0).astype(F32) * fields[b]
            left = jnp.concatenate(halves(from_locals[c]), axis=0)
            right = jnp.concatenate(halves(field.T), axis=1)
            far.append(fold(product(left, right)))
        for c in range(clusters):
            crossed_copies[c].wait_recv()
            held = current[c]
            applied = held + (direct[c] + parity * returned[sweep, c]) + far[c]
            if sweep == ITERS - 1:
                applied_out[c] = applied
                held_out[c] = held
            else:
                iterate[c] = held + DAMPING * (incident[c] - applied)
        if sweep < ITERS - 1:
            moments(iterate, sweep + 1)
            recv_out[sweep + 1, me] = send_out[sweep + 1, me]

    for copy in sent:
        copy.wait_send()


def sweeps(*args):
    incident, near_real, transfer_ops, far_source = args[0], args[1], args[5], args[9]
    n = lax.axis_size("cl")
    clusters, points, width = incident.shape
    near_max = near_real.shape[1]
    kinds, coeffs = transfer_ops.shape[:2]
    boxes, far_max = far_source.shape
    share = width // n
    tiled = n % 2 == 0 and width % n == 0 and share % 16 == 0 and far_max <= 128 and 2 * boxes <= 8
    if not (tiled and ITERS == 2 and points % 128 == 0 and coeffs % 128 == 0 and width % 128 == 0):
        return shards(*args)
    rows = n * boxes * share
    vmem, hbm = (pl.BlockSpec(memory_space=space) for space in (pltpu.VMEM, pl.ANY))
    field = pltpu.VMEM(incident.shape, F32)
    held, applied = (
        pl.pallas_call(
            body,
            out_shape=(field, field),
            in_specs=[hbm] * 12,
            out_specs=(vmem, vmem),
            scratch_shapes=[
                pltpu.VMEM(incident.shape, F32),
                pltpu.VMEM(args[3].shape, F32),
                pltpu.VMEM(args[4].shape, F32),
                pltpu.SMEM(args[6].shape, jnp.int32),
                pltpu.SMEM(args[7].shape, jnp.int32),
                pltpu.SMEM(args[8].shape, jnp.int32),
                pltpu.VMEM(far_source.shape, jnp.int32),
                pltpu.VMEM(far_source.shape, jnp.int32),
                pltpu.SMEM(args[11].shape, jnp.int32),
                pltpu.VMEM((2,) + near_real.shape, F32),
                pltpu.VMEM(transfer_ops.shape, F32),
                pltpu.VMEM((clusters, 4 * points, near_max * points), BF16),
                pltpu.VMEM((clusters, near_max * points, 2 * width), BF16),
                pltpu.VMEM((kinds, coeffs, 2 * coeffs), BF16),
                pltpu.VMEM((kinds, rows, rows), BF16),
                pltpu.VMEM((2, rows, kinds * coeffs), BF16),
                pltpu.VMEM((8, 128), jnp.int32),
                pltpu.VMEM((n, 8, 128), jnp.int32),
                pltpu.VMEM(incident.shape, F32),
                pltpu.VMEM((ITERS, 3 * clusters, points, width), F32),
                pltpu.VMEM((3 * clusters, points, 2 * width), BF16),
                pltpu.VMEM((ITERS, n, boxes * share, coeffs), F32),
                pltpu.VMEM((ITERS, n, boxes * share, coeffs), F32),
                pltpu.VMEM((ITERS, n, boxes * share, coeffs), F32),
                pltpu.VMEM((ITERS, n, boxes * share, coeffs), F32),
                pltpu.VMEM((ITERS,) + incident.shape, F32),
                pltpu.VMEM((ITERS,) + incident.shape, F32),
                pltpu.SemaphoreType.DMA((12,)),
                pltpu.SemaphoreType.DMA((2, 1 + 4 * ITERS, n)),
            ],
            compiler_params=pltpu.CompilerParams(
                collective_id=0, has_side_effects=True, vmem_limit_bytes=60 * 1024 * 1024
            ),
        )(*args)
    )
    residual = incident - applied
    return (held + DAMPING * residual, residual)


def solution(mesh):
    return jax.shard_map(
        sweeps,
        mesh=mesh,
        in_specs=(
            P("cl", None, "grp"),
            P("cl", None, None, None),
            P("cl", None, None, None),
            P("cl", None, None),
            P("cl", None, None),
            P(),
            P("cl", None),
            P("cl"),
            P("cl"),
            P("cl", None),
            P("cl", None),
            P("cl"),
        ),
        out_specs=(P("cl", None, "grp"), P("cl", None, "grp")),
        check_vma=False,
    )
```

```python
import functools

import jax
import jax.numpy as jnp
from jax import lax
from jax.experimental import pallas as pl
from jax.experimental.pallas import tpu as pltpu
from jax.sharding import PartitionSpec as P

ITERS = 2


DAMPING = 0.7


def padded(block, sides, width):
    for axis, dim in sides:
        count = lax.axis_size(axis)
        forward = [(i, i + 1) for i in range(count - 1)]
        forward.append((count - 1, 0))
        backward = [(target, source) for source, target in forward]
        low = lax.ppermute(
            lax.slice_in_dim(block, block.shape[dim] - width, None, axis=dim), axis, forward
        )
        high = lax.ppermute(lax.slice_in_dim(block, 0, width, axis=dim), axis, backward)
        block = jnp.concatenate([low, block, high], axis=dim)
    return block


def partner(x, axis, bit):
    return lax.ppermute(x, axis, [(i, i ^ 1 << bit) for i in range(lax.axis_size(axis))])


def operator_product(form, left, right):
    return jnp.einsum(form, left, right, precision=lax.Precision.HIGHEST)


def shards(
    incident,
    near_real,
    near_imag,
    to_moments,
    from_locals,
    transfer_ops,
    near_index,
    near_count,
    cluster_box,
    far_source,
    far_kind,
    far_count,
):
    per_slab, points, width = incident.shape
    box_count, far_max = far_source.shape
    kind_total, coeffs = (transfer_ops.shape[0], transfer_ops.shape[1])
    near_max = near_index.shape[1]
    parity = jnp.where(lax.axis_index("grp") < lax.axis_size("grp") // 2, -1.0, 1.0).astype(
        jnp.float32
    )
    partner_bit = lax.axis_size("grp").bit_length() - 2
    live_near = (jnp.arange(near_max, dtype=jnp.int32)[None, :] < near_count[:, None]).astype(
        jnp.float32
    )
    window_hot = (
        near_index[:, :, None] == jnp.arange(3 * per_slab, dtype=jnp.int32)
    ).astype(jnp.float32) * live_near[:, :, None]
    box_onehot_matrix = (
        cluster_box[:, None] == jnp.arange(box_count, dtype=jnp.int32)[None, :]
    ).astype(jnp.float32)
    active_far_links = jnp.arange(far_max, dtype=jnp.int32)[None, :] < far_count[:, None]
    kind_hot = (
        (far_kind[:, :, None] == jnp.arange(kind_total, dtype=jnp.int32))
        & active_far_links[:, :, None]
    ).astype(jnp.float32)
    pressure = incident
    residual = jnp.zeros_like(incident)
    for iteration in range(ITERS):
        window = padded(pressure, (("cl", 0),), per_slab)
        surface_panels = operator_product("cew,wqk->ceqk", window_hot, window)
        direct = operator_product("cepq,ceqk->cpk", near_real, surface_panels)
        crossed = operator_product("cepq,ceqk->cpk", near_imag, surface_panels)
        returned = partner(crossed, "grp", partner_bit)
        multipole_series = operator_product("cqp,cpk->cqk", to_moments, pressure)
        moment_values = operator_product("ym,ysw->msw", box_onehot_matrix, multipole_series)
        shard_piece = lax.all_gather(moment_values, "cl", axis=0, tiled=True)
        length_total = shard_piece.shape[0]
        source_hot = (
            far_source[:, :, None] == jnp.arange(length_total, dtype=jnp.int32)[None, None, :]
        ).astype(jnp.float32)
        weights = operator_product("tfj,tfy->tjy", source_hot, kind_hot)
        grouped = operator_product("tjy,jqk->tyqk", weights, shard_piece)
        local_field = operator_product("yrq,tyqk->trk", transfer_ops, grouped)
        cluster_local = operator_product("cb,brk->crk", box_onehot_matrix, local_field)
        applied = (
            pressure
            + (direct + parity * returned)
            + operator_product("cpr,crk->cpk", from_locals, cluster_local)
        )
        residual = incident - applied
        pressure = pressure + DAMPING * residual
    return (pressure, residual)


F32, BF16 = jnp.float32, jnp.bfloat16
MESH = pl.DeviceIdType.MESH


def halves(x):
    high = x.astype(BF16)
    return high, (x - high.astype(F32)).astype(BF16)


def product(left, right):
    return jnp.dot(left, right, preferred_element_type=F32)


def fold(o):
    m, n = o.shape[0] // 2, o.shape[1] // 2
    return o[:m, :n] + (o[:m, n:] + o[m:, :n])


def body(
    incident_in,
    near_real,
    near_imag,
    to_moments_in,
    from_locals_in,
    transfer_ops,
    near_index_in,
    near_count_in,
    cluster_box_in,
    far_source_in,
    far_kind_in,
    far_count_in,
    held_out,
    applied_out,
    incident,
    to_moments,
    from_locals,
    near_index,
    near_count,
    cluster_box,
    far_source,
    far_kind,
    far_count,
    near_raw,
    ops_raw,
    near_rows,
    ops_hl,
    hot,
    grouped,
    info,
    info_all,
    iterate,
    window,
    window_hl,
    send_out,
    recv_out,
    send_home,
    recv_home,
    crossed,
    returned,
    load_sem,
    sems,
):
    n, grps = lax.axis_size("cl"), lax.axis_size("grp")
    me, grp = lax.axis_index("cl"), lax.axis_index("grp")
    clusters, points, width = incident.shape
    boxes, far_max = far_source.shape
    near_max = near_index.shape[1]
    kinds, coeffs = transfer_ops.shape[0], transfer_ops.shape[1]
    share = width // n
    other = lax.rem(grp + grps // 2, grps)
    parity = jnp.where(grp < grps // 2, -1.0, 1.0).astype(F32)
    after, before = lax.rem(me + 1, n), lax.rem(me + n - 1, n)

    barrier = pltpu.get_barrier_semaphore()
    for j in range(1, n):
        pl.semaphore_signal(barrier, inc=1, device_id={"cl": lax.rem(me + j, n)}, device_id_type=MESH)
    pl.semaphore_signal(barrier, inc=1, device_id={"grp": other}, device_id_type=MESH)

    pairs = (
        (transfer_ops, ops_raw),
        (near_real, near_raw.at[0]),
        (near_imag, near_raw.at[1]),
        (incident_in, incident),
        (to_moments_in, to_moments),
        (cluster_box_in, cluster_box),
        (far_source_in, far_source),
        (far_kind_in, far_kind),
        (far_count_in, far_count),
        (from_locals_in, from_locals),
        (near_index_in, near_index),
        (near_count_in, near_count),
    )
    loads = [
        pltpu.make_async_copy(source, target, load_sem.at[at])
        for at, (source, target) in enumerate(pairs)
    ]
    for load in loads[3:] + loads[:3]:
        load.start()

    sent = []

    def remote(source, target, kind, j, device, slot=None):
        copy = pltpu.make_async_remote_copy(
            src_ref=source,
            dst_ref=target,
            send_sem=sems.at[0, kind, j],
            recv_sem=sems.at[1, kind, j if slot is None else slot],
            device_id=device,
            device_id_type=MESH,
        )
        copy.start()
        sent.append(copy)
        return copy

    quads = n // 2
    side = me // quads

    def deliver(source, target, kind, turn):
        block = 1 - side if turn == 0 else side
        for i in range(turn, quads):
            if turn == 0:
                at = i + (1 - side) * (quads - 1 - 2 * i)
            else:
                at = lax.rem(me + i, quads)
            peer = block * quads + at
            j = (1 - turn) * quads + i
            remote(source.at[peer], target.at[me], kind, j, {"cl": peer}, me)

    def collect(target, kind):
        for j in range(1, n):
            sender = lax.rem(me + j, n)
            pltpu.make_async_remote_copy(
                src_ref=target.at[sender],
                dst_ref=target.at[sender],
                send_sem=sems.at[0, kind, j],
                recv_sem=sems.at[1, kind, sender],
                device_id={"cl": sender},
                device_id_type=MESH,
            ).wait_recv()

    def moments(current, sweep):
        parts = []
        for c in range(clusters):
            left = jnp.concatenate(halves(to_moments[c]), axis=0)
            right = jnp.concatenate(halves(current[c]), axis=1)
            parts.append(fold(product(left, right)).T)
        for b in range(boxes):
            total = jnp.zeros((width, coeffs), F32)
            for c in range(clusters):
                total = total + jnp.where(cluster_box[c] == b, 1.0, 0.0).astype(F32) * parts[c]
            for d in range(n):
                send_out[sweep, d, b * share : (b + 1) * share, :] = total[d * share : (d + 1) * share, :]

    for load in loads[3:]:
        load.wait()
    info[...] = jnp.full(info.shape, -1, jnp.int32)
    lane = lax.broadcasted_iota(jnp.int32, (1, far_max), 1)
    for b in range(boxes):
        info[b : b + 1, 0:far_max] = far_source[b : b + 1, :]
        info[boxes + b : boxes + b + 1, 0:far_max] = jnp.where(
            lane < far_count[b], far_kind[b : b + 1, :], -1
        )
    info_all[me] = info[...]
    moments(incident, 0)
    recv_out[0, me] = send_out[0, me]

    pl.semaphore_wait(barrier, n)
    info_copies = [
        remote(info, info_all.at[me], 0, j, {"cl": lax.rem(me + j, n)}) for j in range(1, n)
    ]

    for sweep in range(ITERS):
        current = incident if sweep == 0 else iterate
        base = 1 + sweep * 4
        odd = lax.rem(me, 2)
        slab = window.at[sweep]
        window_copies = []

        def widen(place):
            window_copies.append(
                remote(
                    current,
                    slab.at[pl.ds(2 * clusters * place, clusters)],
                    base + 1,
                    place,
                    {"cl": place * before + (1 - place) * after},
                )
            )

        ahead = sweep in (1,)
        deliver(send_out.at[sweep], recv_out.at[sweep], base, 0)
        if ahead:
            widen(1 - odd)
        deliver(send_out.at[sweep], recv_out.at[sweep], base, 1)
        if not ahead:
            widen(1 - odd)
        widen(odd)
        if sweep == 0:
            loads[0].wait()

            @pl.loop(0, kinds)
            def _(kind):
                turned = ops_raw[kind].T
                high, low = halves(turned)
                ops_hl[kind, :, 0:coeffs] = high
                ops_hl[kind, :, coeffs : 2 * coeffs] = low

            loads[1].wait()
            loads[2].wait()
            for part in range(2):
                for c in range(clusters):
                    for e in range(near_max):
                        live = jnp.where(e < near_count[c], 1.0, 0.0).astype(F32)
                        high, low = halves(near_raw[part, c, e] * live)
                        cols = slice(e * points, (e + 1) * points)
                        at = (2 - 2 * part) * points
                        near_rows[c, at : at + points, cols] = high
                        near_rows[c, at + points : at + 2 * points, cols] = low
            for copy in info_copies:
                copy.wait_recv()
            rows = n * boxes * share
            kind_id = lax.broadcasted_iota(jnp.int32, (kinds, info.shape[1]), 0)
            source_id = lax.broadcasted_iota(jnp.int32, (rows, info.shape[1]), 0) // share
            same = (
                lax.broadcasted_iota(jnp.int32, (share, rows), 1) % share
                == lax.broadcasted_iota(jnp.int32, (share, rows), 0)
            )
            same = jnp.where(same, 1.0, 0.0).astype(F32)
            for d in range(n):
                for b in range(boxes):
                    of_kind = jnp.where(info_all[d, boxes + b : boxes + b + 1, :] == kind_id, 1.0, 0.0)
                    of_source = jnp.where(info_all[d, b : b + 1, :] == source_id, 1.0, 0.0)
                    weight = lax.dot_general(
                        of_kind.astype(BF16),
                        of_source.astype(BF16),
                        (((1,), (1,)), ((), ())),
                        preferred_element_type=F32,
                    )
                    spread = weight[:, None, :] * same[None, :, :]
                    at = (d * boxes + b) * share
                    hot[:, at : at + share, :] = spread.astype(BF16)

        collect(recv_out.at[sweep], base)
        series = recv_out[sweep].reshape(n * boxes * share, coeffs)
        series_hl = jnp.concatenate(halves(series), axis=1)
        rows = n * boxes * share
        few = rows // 2
        for turn in range(2):
            block = 1 - side if turn == 0 else side
            first = pl.multiple_of(block * few, few)
            for kind in range(kinds):
                both = product(hot[kind, pl.ds(first, few), :], series_hl)
                high, low = halves(both[:, :coeffs] + both[:, coeffs:])
                cols = slice(kind * coeffs, (kind + 1) * coeffs)
                grouped[turn, 0:few, cols] = high
                grouped[turn, few : 2 * few, cols] = low
            local = fold(product(grouped[turn], ops_hl[...].reshape(kinds * coeffs, 2 * coeffs)))
            local = local.reshape(quads, boxes * share, coeffs)
            send_home[sweep, pl.ds(block * quads, quads)] = local
            deliver(send_home.at[sweep], recv_home.at[sweep], base + 2, turn)
        recv_home[sweep, me] = send_home[sweep, me]

        for w in range(clusters):
            high, low = halves(current[w])
            window_hl[clusters + w, :, 0:width] = high
            window_hl[clusters + w, :, width : 2 * width] = low
        for copy in window_copies:
            copy.wait_recv()
        for w in list(range(clusters)) + list(range(2 * clusters, 3 * clusters)):
            high, low = halves(window[sweep, w])
            window_hl[w, :, 0:width] = high
            window_hl[w, :, width : 2 * width] = low
        direct, crossed_copies = [], []

        def near_sum(c, row):
            total = None
            for e in range(0, near_max, 4):
                panel = jnp.concatenate(
                    [window_hl[near_index[c, e + k]] for k in range(4)], axis=0
                )
                cols = slice(e * points, (e + 4) * points)
                term = product(near_rows[c, row : row + 2 * points, cols], panel)
                total = term if total is None else total + term
            return total

        for c in range(clusters):
            crossed[sweep, c] = fold(near_sum(c, 0))
            crossed_copies.append(
                remote(crossed.at[sweep, c], returned.at[sweep, c], base + 3, c, {"grp": other})
            )
        for c in range(clusters):
            direct.append(fold(near_sum(c, 2 * points)))

        collect(recv_home.at[sweep], base + 2)
        fields = [
            jnp.concatenate(
                [recv_home[sweep, d, b * share : (b + 1) * share, :] for d in range(n)], axis=0
            )
            for b in range(boxes)
        ]
        far = []
        for c in range(clusters):
            field = jnp.zeros((width, coeffs), F32)
            for b in range(boxes):
                field = field + jnp.where(cluster_box[c] == b, 1.0, 0.0).astype(F32) * fields[b]
            left = jnp.concatenate(halves(from_locals[c]), axis=0)
            right = jnp.concatenate(halves(field.T), axis=1)
            far.append(fold(product(left, right)))
        for c in range(clusters):
            crossed_copies[c].wait_recv()
            held = current[c]
            applied = held + (direct[c] + parity * returned[sweep, c]) + far[c]
            if sweep == ITERS - 1:
                applied_out[c] = applied
                held_out[c] = held
            else:
                iterate[c] = held + DAMPING * (incident[c] - applied)
        if sweep < ITERS - 1:
            moments(iterate, sweep + 1)
            recv_out[sweep + 1, me] = send_out[sweep + 1, me]

    for copy in sent:
        copy.wait_send()


def sweeps(*args):
    incident, near_real, transfer_ops, far_source = args[0], args[1], args[5], args[9]
    n = lax.axis_size("cl")
    clusters, points, width = incident.shape
    near_max = near_real.shape[1]
    kinds, coeffs = transfer_ops.shape[:2]
    boxes, far_max = far_source.shape
    share = width // n
    tiled = n % 2 == 0 and near_max % 4 == 0 and width % n == 0 and share % 16 == 0 and far_max <= 128 and 2 * boxes <= 8
    if not (tiled and ITERS == 2 and points % 128 == 0 and coeffs % 128 == 0 and width % 128 == 0):
        return shards(*args)
    rows = n * boxes * share
    vmem, hbm = (pl.BlockSpec(memory_space=space) for space in (pltpu.VMEM, pl.ANY))
    field = pltpu.VMEM(incident.shape, F32)
    held, applied = (
        pl.pallas_call(
            body,
            out_shape=(field, field),
            in_specs=[hbm] * 12,
            out_specs=(vmem, vmem),
            scratch_shapes=[
                pltpu.VMEM(incident.shape, F32),
                pltpu.VMEM(args[3].shape, F32),
                pltpu.VMEM(args[4].shape, F32),
                pltpu.SMEM(args[6].shape, jnp.int32),
                pltpu.SMEM(args[7].shape, jnp.int32),
                pltpu.SMEM(args[8].shape, jnp.int32),
                pltpu.VMEM(far_source.shape, jnp.int32),
                pltpu.VMEM(far_source.shape, jnp.int32),
                pltpu.SMEM(args[11].shape, jnp.int32),
                pltpu.VMEM((2,) + near_real.shape, F32),
                pltpu.VMEM(transfer_ops.shape, F32),
                pltpu.VMEM((clusters, 4 * points, near_max * points), BF16),
                pltpu.VMEM((kinds, coeffs, 2 * coeffs), BF16),
                pltpu.VMEM((kinds, rows, rows), BF16),
                pltpu.VMEM((2, rows, kinds * coeffs), BF16),
                pltpu.VMEM((8, 128), jnp.int32),
                pltpu.VMEM((n, 8, 128), jnp.int32),
                pltpu.VMEM(incident.shape, F32),
                pltpu.VMEM((ITERS, 3 * clusters, points, width), F32),
                pltpu.VMEM((3 * clusters, points, 2 * width), BF16),
                pltpu.VMEM((ITERS, n, boxes * share, coeffs), F32),
                pltpu.VMEM((ITERS, n, boxes * share, coeffs), F32),
                pltpu.VMEM((ITERS, n, boxes * share, coeffs), F32),
                pltpu.VMEM((ITERS, n, boxes * share, coeffs), F32),
                pltpu.VMEM((ITERS,) + incident.shape, F32),
                pltpu.VMEM((ITERS,) + incident.shape, F32),
                pltpu.SemaphoreType.DMA((12,)),
                pltpu.SemaphoreType.DMA((2, 1 + 4 * ITERS, n)),
            ],
            compiler_params=pltpu.CompilerParams(
                collective_id=0, has_side_effects=True, vmem_limit_bytes=60 * 1024 * 1024
            ),
        )(*args)
    )
    residual = incident - applied
    return (held + DAMPING * residual, residual)


def solution(mesh):
    return jax.shard_map(
        sweeps,
        mesh=mesh,
        in_specs=(
            P("cl", None, "grp"),
            P("cl", None, None, None),
            P("cl", None, None, None),
            P("cl", None, None),
            P("cl", None, None),
            P(),
            P("cl", None),
            P("cl"),
            P("cl"),
            P("cl", None),
            P("cl", None),
            P("cl"),
        ),
        out_specs=(P("cl", None, "grp"), P("cl", None, "grp")),
        check_vma=False,
    )
```

```python
import functools

import jax
import jax.numpy as jnp
from jax import lax
from jax.experimental import pallas as pl
from jax.experimental.pallas import tpu as pltpu
from jax.sharding import PartitionSpec as P

ITERS = 2


DAMPING = 0.7


def padded(block, sides, width):
    for axis, dim in sides:
        count = lax.axis_size(axis)
        forward = [(i, i + 1) for i in range(count - 1)]
        forward.append((count - 1, 0))
        backward = [(target, source) for source, target in forward]
        low = lax.ppermute(
            lax.slice_in_dim(block, block.shape[dim] - width, None, axis=dim), axis, forward
        )
        high = lax.ppermute(lax.slice_in_dim(block, 0, width, axis=dim), axis, backward)
        block = jnp.concatenate([low, block, high], axis=dim)
    return block


def partner(x, axis, bit):
    return lax.ppermute(x, axis, [(i, i ^ 1 << bit) for i in range(lax.axis_size(axis))])


def operator_product(form, left, right):
    return jnp.einsum(form, left, right, precision=lax.Precision.HIGHEST)


def shards(
    incident,
    near_real,
    near_imag,
    to_moments,
    from_locals,
    transfer_ops,
    near_index,
    near_count,
    cluster_box,
    far_source,
    far_kind,
    far_count,
):
    per_slab, points, width = incident.shape
    box_count, far_max = far_source.shape
    kind_total, coeffs = (transfer_ops.shape[0], transfer_ops.shape[1])
    near_max = near_index.shape[1]
    parity = jnp.where(lax.axis_index("grp") < lax.axis_size("grp") // 2, -1.0, 1.0).astype(
        jnp.float32
    )
    partner_bit = lax.axis_size("grp").bit_length() - 2
    live_near = (jnp.arange(near_max, dtype=jnp.int32)[None, :] < near_count[:, None]).astype(
        jnp.float32
    )
    window_hot = (
        near_index[:, :, None] == jnp.arange(3 * per_slab, dtype=jnp.int32)
    ).astype(jnp.float32) * live_near[:, :, None]
    box_onehot_matrix = (
        cluster_box[:, None] == jnp.arange(box_count, dtype=jnp.int32)[None, :]
    ).astype(jnp.float32)
    active_far_links = jnp.arange(far_max, dtype=jnp.int32)[None, :] < far_count[:, None]
    kind_hot = (
        (far_kind[:, :, None] == jnp.arange(kind_total, dtype=jnp.int32))
        & active_far_links[:, :, None]
    ).astype(jnp.float32)
    pressure = incident
    residual = jnp.zeros_like(incident)
    for iteration in range(ITERS):
        window = padded(pressure, (("cl", 0),), per_slab)
        surface_panels = operator_product("cew,wqk->ceqk", window_hot, window)
        direct = operator_product("cepq,ceqk->cpk", near_real, surface_panels)
        crossed = operator_product("cepq,ceqk->cpk", near_imag, surface_panels)
        returned = partner(crossed, "grp", partner_bit)
        multipole_series = operator_product("cqp,cpk->cqk", to_moments, pressure)
        moment_values = operator_product("ym,ysw->msw", box_onehot_matrix, multipole_series)
        shard_piece = lax.all_gather(moment_values, "cl", axis=0, tiled=True)
        length_total = shard_piece.shape[0]
        source_hot = (
            far_source[:, :, None] == jnp.arange(length_total, dtype=jnp.int32)[None, None, :]
        ).astype(jnp.float32)
        weights = operator_product("tfj,tfy->tjy", source_hot, kind_hot)
        grouped = operator_product("tjy,jqk->tyqk", weights, shard_piece)
        local_field = operator_product("yrq,tyqk->trk", transfer_ops, grouped)
        cluster_local = operator_product("cb,brk->crk", box_onehot_matrix, local_field)
        applied = (
            pressure
            + (direct + parity * returned)
            + operator_product("cpr,crk->cpk", from_locals, cluster_local)
        )
        residual = incident - applied
        pressure = pressure + DAMPING * residual
    return (pressure, residual)


F32, BF16 = jnp.float32, jnp.bfloat16
MESH = pl.DeviceIdType.MESH


def halves(x):
    high = x.astype(BF16)
    return high, (x - high.astype(F32)).astype(BF16)


def product(left, right):
    return jnp.dot(left, right, preferred_element_type=F32)


def fold(o):
    m, n = o.shape[0] // 2, o.shape[1] // 2
    return o[:m, :n] + (o[:m, n:] + o[m:, :n])


def body(
    incident_in,
    near_real,
    near_imag,
    to_moments_in,
    from_locals_in,
    transfer_ops,
    near_index_in,
    near_count_in,
    cluster_box_in,
    far_source_in,
    far_kind_in,
    far_count_in,
    held_out,
    applied_out,
    incident,
    to_moments,
    from_locals,
    near_index,
    near_count,
    cluster_box,
    far_source,
    far_kind,
    far_count,
    near_raw,
    ops_raw,
    near_rows,
    ops_hl,
    hot,
    grouped,
    info,
    info_all,
    iterate,
    window,
    window_hl,
    send_out,
    recv_out,
    send_home,
    recv_home,
    crossed,
    returned,
    load_sem,
    sems,
):
    n, grps = lax.axis_size("cl"), lax.axis_size("grp")
    me, grp = lax.axis_index("cl"), lax.axis_index("grp")
    clusters, points, width = incident.shape
    boxes, far_max = far_source.shape
    near_max = near_index.shape[1]
    kinds, coeffs = transfer_ops.shape[0], transfer_ops.shape[1]
    share = width // n
    other = lax.rem(grp + grps // 2, grps)
    parity = jnp.where(grp < grps // 2, -1.0, 1.0).astype(F32)
    after, before = lax.rem(me + 1, n), lax.rem(me + n - 1, n)

    barrier = pltpu.get_barrier_semaphore()
    for j in sorted(range(1, n), key=lambda j: -min(j, n - j)):
        pl.semaphore_signal(barrier, inc=1, device_id={"cl": lax.rem(me + j, n)}, device_id_type=MESH)
    pl.semaphore_signal(barrier, inc=1, device_id={"grp": other}, device_id_type=MESH)

    pairs = (
        (transfer_ops, ops_raw),
        (near_real, near_raw.at[0]),
        (near_imag, near_raw.at[1]),
        (incident_in, incident),
        (to_moments_in, to_moments),
        (cluster_box_in, cluster_box),
        (far_source_in, far_source),
        (far_kind_in, far_kind),
        (far_count_in, far_count),
        (from_locals_in, from_locals),
        (near_index_in, near_index),
        (near_count_in, near_count),
    )
    loads = [
        pltpu.make_async_copy(source, target, load_sem.at[at])
        for at, (source, target) in enumerate(pairs)
    ]
    for load in loads[3:] + loads[:3]:
        load.start()

    sent = []

    def remote(source, target, kind, j, device, slot=None):
        copy = pltpu.make_async_remote_copy(
            src_ref=source,
            dst_ref=target,
            send_sem=sems.at[0, kind, j],
            recv_sem=sems.at[1, kind, j if slot is None else slot],
            device_id=device,
            device_id_type=MESH,
        )
        copy.start()
        sent.append(copy)
        return copy

    quads = n // 2
    side = me // quads

    def deliver(source, target, kind, turn):
        block = 1 - side if turn == 0 else side
        for i in range(turn, quads):
            if turn == 0:
                at = i + (1 - side) * (quads - 1 - 2 * i)
            else:
                at = lax.rem(me + i, quads)
            peer = block * quads + at
            j = (1 - turn) * quads + i
            remote(source.at[peer], target.at[me], kind, j, {"cl": peer}, me)

    def collect(target, kind):
        for j in range(1, n):
            sender = lax.rem(me + j, n)
            pltpu.make_async_remote_copy(
                src_ref=target.at[sender],
                dst_ref=target.at[sender],
                send_sem=sems.at[0, kind, j],
                recv_sem=sems.at[1, kind, sender],
                device_id={"cl": sender},
                device_id_type=MESH,
            ).wait_recv()

    def moments(current, sweep):
        parts = []
        for c in range(clusters):
            left = jnp.concatenate(halves(to_moments[c]), axis=0)
            right = jnp.concatenate(halves(current[c]), axis=1)
            parts.append(fold(product(left, right)).T)
        for b in range(boxes):
            total = jnp.zeros((width, coeffs), F32)
            for c in range(clusters):
                total = total + jnp.where(cluster_box[c] == b, 1.0, 0.0).astype(F32) * parts[c]
            for d in range(n):
                send_out[sweep, d, b * share : (b + 1) * share, :] = total[d * share : (d + 1) * share, :]

    for load in loads[3:]:
        load.wait()
    info[...] = jnp.full(info.shape, -1, jnp.int32)
    lane = lax.broadcasted_iota(jnp.int32, (1, far_max), 1)
    for b in range(boxes):
        info[b : b + 1, 0:far_max] = far_source[b : b + 1, :]
        info[boxes + b : boxes + b + 1, 0:far_max] = jnp.where(
            lane < far_count[b], far_kind[b : b + 1, :], -1
        )
    info_all[me] = info[...]
    moments(incident, 0)
    recv_out[0, me] = send_out[0, me]

    pl.semaphore_wait(barrier, n)
    info_copies = [
        remote(info, info_all.at[me], 0, j, {"cl": lax.rem(me + j, n)}) for j in range(1, n)
    ]

    for sweep in range(ITERS):
        current = incident if sweep == 0 else iterate
        base = 1 + sweep * 4
        odd = lax.rem(me, 2)
        slab = window.at[sweep]
        window_copies = []

        def widen(place):
            window_copies.append(
                remote(
                    current,
                    slab.at[pl.ds(2 * clusters * place, clusters)],
                    base + 1,
                    place,
                    {"cl": place * before + (1 - place) * after},
                )
            )

        ahead = sweep in (1,)
        deliver(send_out.at[sweep], recv_out.at[sweep], base, 0)
        if ahead:
            widen(1 - odd)
        deliver(send_out.at[sweep], recv_out.at[sweep], base, 1)
        if not ahead:
            widen(1 - odd)
        widen(odd)
        if sweep == 0:
            loads[0].wait()

            @pl.loop(0, kinds)
            def _(kind):
                turned = ops_raw[kind].T
                high, low = halves(turned)
                ops_hl[kind, :, 0:coeffs] = high
                ops_hl[kind, :, coeffs : 2 * coeffs] = low

            loads[1].wait()
            loads[2].wait()
            for part in range(2):
                for c in range(clusters):
                    for e in range(near_max):
                        live = jnp.where(e < near_count[c], 1.0, 0.0).astype(F32)
                        high, low = halves(near_raw[part, c, e] * live)
                        cols = slice(e * points, (e + 1) * points)
                        at = (2 - 2 * part) * points
                        near_rows[c, at : at + points, cols] = high
                        near_rows[c, at + points : at + 2 * points, cols] = low
            for copy in info_copies:
                copy.wait_recv()
            rows = n * boxes * share
            kind_id = lax.broadcasted_iota(jnp.int32, (kinds, info.shape[1]), 0)
            source_id = lax.broadcasted_iota(jnp.int32, (rows, info.shape[1]), 0) // share
            same = (
                lax.broadcasted_iota(jnp.int32, (share, rows), 1) % share
                == lax.broadcasted_iota(jnp.int32, (share, rows), 0)
            )
            same = jnp.where(same, 1.0, 0.0).astype(F32)
            for d in range(n):
                for b in range(boxes):
                    of_kind = jnp.where(info_all[d, boxes + b : boxes + b + 1, :] == kind_id, 1.0, 0.0)
                    of_source = jnp.where(info_all[d, b : b + 1, :] == source_id, 1.0, 0.0)
                    weight = lax.dot_general(
                        of_kind.astype(BF16),
                        of_source.astype(BF16),
                        (((1,), (1,)), ((), ())),
                        preferred_element_type=F32,
                    )
                    spread = weight[:, None, :] * same[None, :, :]
                    at = (d * boxes + b) * share
                    hot[:, at : at + share, :] = spread.astype(BF16)

        collect(recv_out.at[sweep], base)
        series = recv_out[sweep].reshape(n * boxes * share, coeffs)
        series_hl = jnp.concatenate(halves(series), axis=1)
        rows = n * boxes * share
        few = rows // 2
        for turn in range(2):
            block = 1 - side if turn == 0 else side
            first = pl.multiple_of(block * few, few)
            for kind in range(kinds):
                both = product(hot[kind, pl.ds(first, few), :], series_hl)
                high, low = halves(both[:, :coeffs] + both[:, coeffs:])
                cols = slice(kind * coeffs, (kind + 1) * coeffs)
                grouped[turn, 0:few, cols] = high
                grouped[turn, few : 2 * few, cols] = low
            local = fold(product(grouped[turn], ops_hl[...].reshape(kinds * coeffs, 2 * coeffs)))
            local = local.reshape(quads, boxes * share, coeffs)
            send_home[sweep, pl.ds(block * quads, quads)] = local
            deliver(send_home.at[sweep], recv_home.at[sweep], base + 2, turn)
        recv_home[sweep, me] = send_home[sweep, me]

        for w in range(clusters):
            high, low = halves(current[w])
            window_hl[clusters + w, :, 0:width] = high
            window_hl[clusters + w, :, width : 2 * width] = low
        for copy in window_copies:
            copy.wait_recv()
        for w in list(range(clusters)) + list(range(2 * clusters, 3 * clusters)):
            high, low = halves(window[sweep, w])
            window_hl[w, :, 0:width] = high
            window_hl[w, :, width : 2 * width] = low
        direct, crossed_copies = [], []

        def near_sum(c, row):
            total = None
            for e in range(0, near_max, 4):
                panel = jnp.concatenate(
                    [window_hl[near_index[c, e + k]] for k in range(4)], axis=0
                )
                cols = slice(e * points, (e + 4) * points)
                term = product(near_rows[c, row : row + 2 * points, cols], panel)
                total = term if total is None else total + term
            return total

        for c in range(clusters):
            crossed[sweep, c] = fold(near_sum(c, 0))
            crossed_copies.append(
                remote(crossed.at[sweep, c], returned.at[sweep, c], base + 3, c, {"grp": other})
            )
        for c in range(clusters):
            direct.append(fold(near_sum(c, 2 * points)))

        collect(recv_home.at[sweep], base + 2)
        fields = [
            jnp.concatenate(
                [recv_home[sweep, d, b * share : (b + 1) * share, :] for d in range(n)], axis=0
            )
            for b in range(boxes)
        ]
        far = []
        for c in range(clusters):
            field = jnp.zeros((width, coeffs), F32)
            for b in range(boxes):
                field = field + jnp.where(cluster_box[c] == b, 1.0, 0.0).astype(F32) * fields[b]
            left = jnp.concatenate(halves(from_locals[c]), axis=0)
            right = jnp.concatenate(halves(field.T), axis=1)
            far.append(fold(product(left, right)))
        for c in range(clusters):
            crossed_copies[c].wait_recv()
            held = current[c]
            applied = held + (direct[c] + parity * returned[sweep, c]) + far[c]
            if sweep == ITERS - 1:
                applied_out[c] = applied
                held_out[c] = held
            else:
                iterate[c] = held + DAMPING * (incident[c] - applied)
        if sweep < ITERS - 1:
            moments(iterate, sweep + 1)
            recv_out[sweep + 1, me] = send_out[sweep + 1, me]

    for copy in sent:
        copy.wait_send()


def sweeps(*args):
    incident, near_real, transfer_ops, far_source = args[0], args[1], args[5], args[9]
    n = lax.axis_size("cl")
    clusters, points, width = incident.shape
    near_max = near_real.shape[1]
    kinds, coeffs = transfer_ops.shape[:2]
    boxes, far_max = far_source.shape
    share = width // n
    tiled = n % 2 == 0 and near_max % 4 == 0 and width % n == 0 and share % 16 == 0 and far_max <= 128 and 2 * boxes <= 8
    if not (tiled and ITERS == 2 and points % 128 == 0 and coeffs % 128 == 0 and width % 128 == 0):
        return shards(*args)
    rows = n * boxes * share
    vmem, hbm = (pl.BlockSpec(memory_space=space) for space in (pltpu.VMEM, pl.ANY))
    field = pltpu.VMEM(incident.shape, F32)
    held, applied = (
        pl.pallas_call(
            body,
            out_shape=(field, field),
            in_specs=[hbm] * 12,
            out_specs=(vmem, vmem),
            scratch_shapes=[
                pltpu.VMEM(incident.shape, F32),
                pltpu.VMEM(args[3].shape, F32),
                pltpu.VMEM(args[4].shape, F32),
                pltpu.SMEM(args[6].shape, jnp.int32),
                pltpu.SMEM(args[7].shape, jnp.int32),
                pltpu.SMEM(args[8].shape, jnp.int32),
                pltpu.VMEM(far_source.shape, jnp.int32),
                pltpu.VMEM(far_source.shape, jnp.int32),
                pltpu.SMEM(args[11].shape, jnp.int32),
                pltpu.VMEM((2,) + near_real.shape, F32),
                pltpu.VMEM(transfer_ops.shape, F32),
                pltpu.VMEM((clusters, 4 * points, near_max * points), BF16),
                pltpu.VMEM((kinds, coeffs, 2 * coeffs), BF16),
                pltpu.VMEM((kinds, rows, rows), BF16),
                pltpu.VMEM((2, rows, kinds * coeffs), BF16),
                pltpu.VMEM((8, 128), jnp.int32),
                pltpu.VMEM((n, 8, 128), jnp.int32),
                pltpu.VMEM(incident.shape, F32),
                pltpu.VMEM((ITERS, 3 * clusters, points, width), F32),
                pltpu.VMEM((3 * clusters, points, 2 * width), BF16),
                pltpu.VMEM((ITERS, n, boxes * share, coeffs), F32),
                pltpu.VMEM((ITERS, n, boxes * share, coeffs), F32),
                pltpu.VMEM((ITERS, n, boxes * share, coeffs), F32),
                pltpu.VMEM((ITERS, n, boxes * share, coeffs), F32),
                pltpu.VMEM((ITERS,) + incident.shape, F32),
                pltpu.VMEM((ITERS,) + incident.shape, F32),
                pltpu.SemaphoreType.DMA((12,)),
                pltpu.SemaphoreType.DMA((2, 1 + 4 * ITERS, n)),
            ],
            compiler_params=pltpu.CompilerParams(
                collective_id=0, has_side_effects=True, vmem_limit_bytes=60 * 1024 * 1024
            ),
        )(*args)
    )
    residual = incident - applied
    return (held + DAMPING * residual, residual)


def solution(mesh):
    return jax.shard_map(
        sweeps,
        mesh=mesh,
        in_specs=(
            P("cl", None, "grp"),
            P("cl", None, None, None),
            P("cl", None, None, None),
            P("cl", None, None),
            P("cl", None, None),
            P(),
            P("cl", None),
            P("cl"),
            P("cl"),
            P("cl", None),
            P("cl", None),
            P("cl"),
        ),
        out_specs=(P("cl", None, "grp"), P("cl", None, "grp")),
        check_vma=False,
    )
```
